128 devices in a mesh: ctx: 32 (over x_lo, y, z), tp: 4 (over x_hi, core).
Axes of the slice: x: 4 (x_hi: 2, x_lo: 2; x = x_hi * 2 + x_lo), y: 4, z: 4, core: 2. Of those that a mesh axis runs over, the one named last changes fastest.
Arguments:
- query_rows: bfloat16 [16384, 2048], P('ctx', 'tp'), may hold values from -5 to 5
- key_rows: bfloat16 [16384, 1024], P('ctx', 'tp'), may hold values from -5 to 5
- value_rows: bfloat16 [16384, 1024], P('ctx', 'tp'), may hold values from -6 to 6
Outputs:
- attended: bfloat16 [16384, 2048], P(('ctx', 'tp'))
The draws below stay inside these ranges and needn't reach their ends.
All inputs are finite; a program needn't handle non-finite values.
Results may differ from the reference program's by a relative error of at most 0.009.
Values may be sent and summed in bfloat16 or wider, within the bound.
No kernel may reach another device: no remote copies, remote signals or barrier semaphores. Data moves between devices by JAX's collectives and lax.ppermute only.
A program may use at most 192 MiB of HBM per device.

```python
import math
import jax
import jax.numpy as jnp
from jax import lax

HEADS = 16
KV_HEADS = 8
HEAD_DIM = 128
SCALAR = 168
SEQ = 16384


def draw_query_rows(key, part):
    noise_key = jax.random.fold_in(key, 1)
    width = HEADS * HEAD_DIM
    noise = jnp.clip(2.0 * jax.random.normal(noise_key, (SEQ, width), jnp.float32), -5.0, 5.0)
    return noise.astype(jnp.bfloat16)


def draw_key_rows(key, part):
    noise_key = jax.random.fold_in(key, 2)
    width = KV_HEADS * HEAD_DIM
    noise = jnp.clip(jax.random.normal(noise_key, (SEQ, width), jnp.float32), -5.0, 5.0)
    return noise.astype(jnp.bfloat16)


def block_levels(key, dims, cuts, smallest, top_value):
    def one(axis_at, shards_of):
        draws = jax.random.uniform(jax.random.fold_in(jax.random.fold_in(key, 6), axis_at), (shards_of,), jnp.float32, smallest / len(cuts), top_value / len(cuts))
        return jnp.repeat(jnp.exp(draws), dims[axis_at] // shards_of).reshape((-1,) + (1,) * (len(dims) - axis_at - 1))

    loudness = one(*cuts[0])
    for cut in cuts[1:]:
        loudness = loudness * one(*cut)
    return loudness


def gaussian(key, dims, spread, reach, pieces=(), dtype=jnp.bfloat16):
    gain = block_levels(key, dims, pieces, -0.22, 0.18) if pieces else 1.0
    values = jax.random.normal(key, dims, jnp.float32) * spread * gain
    return jnp.minimum(jnp.maximum(values, -reach), reach).astype(dtype)


def setup_inputs(seed: int = 0) -> dict:
    keys = jax.random.split(jax.random.key(seed), 4)
    query_rows = draw_query_rows(jax.random.fold_in(keys[3], 71), 0)
    key_rows = draw_key_rows(jax.random.fold_in(keys[3], 71), 0)
    value_rows = gaussian(keys[2], (SEQ, KV_HEADS * HEAD_DIM), 1.0, 6.0, ((0, 32), (1, 4)))
    return dict(query_rows=query_rows, key_rows=key_rows, value_rows=value_rows)


def reference(query_rows, key_rows, value_rows):
    scaling = SCALAR ** -0.5
    group_size = HEADS // KV_HEADS
    block_len = math.gcd(SEQ, 2048)
    results = []
    for block_start in range(0, SEQ, block_len):
        block_end = block_start + block_len
        q_block = query_rows[block_start:block_end].astype(jnp.float32)
        q_block = q_block.reshape(block_len, KV_HEADS, group_size, HEAD_DIM).transpose(1, 2, 0, 3)
        k_block = key_rows[:block_end].astype(jnp.float32).reshape(block_end, KV_HEADS, HEAD_DIM).transpose(1, 0, 2)
        v_block = value_rows[:block_end].astype(jnp.float32).reshape(block_end, KV_HEADS, HEAD_DIM).transpose(1, 0, 2)
        causal = jnp.arange(block_end)[None, :] <= (block_start + jnp.arange(block_len))[:, None]

        def per_head(operands):
            q_head, k_head, v_head = operands
            scores = jnp.einsum("gqd,kd->gqk", q_head, k_head) * scaling
            scores = jnp.where(causal[None], scores, -1e30)
            peak = jnp.max(scores, axis=-1, keepdims=True)
            weights = jnp.where(causal[None], jnp.exp(scores - peak), 0.0)
            totals = jnp.sum(weights, axis=-1, keepdims=True)
            rounded = lax.optimization_barrier(weights.astype(jnp.bfloat16)).astype(jnp.float32)
            return jnp.einsum("gqk,kd->gqd", rounded, v_head) / totals

        mixed = lax.map(per_head, (q_block, k_block, v_block))
        results.append(mixed.transpose(2, 0, 1, 3).reshape(block_len, HEADS * HEAD_DIM).astype(jnp.bfloat16))
    return jnp.concatenate(results, axis=0)
```

```python
import jax
import jax.numpy as jnp
from jax import lax
from jax.experimental import pallas as pl
from jax.experimental.pallas import tpu as pltpu
from jax.sharding import Mesh, PartitionSpec as P

HEAD_DIM = 128
SCALAR = 168
SCALE = SCALAR ** (-0.5) * 1.4426950408889634
LOWEST = -1e30
BLOCK = 512
ROWS = 2 * BLOCK
EXT = HEAD_DIM + 16

CONTRACT_LAST = (((1,), (1,)), ((), ()))
PARAMS = pltpu.CompilerParams(vmem_limit_bytes=52 * 2**20)


def vmem(count):
    return [pl.BlockSpec(memory_space=pltpu.VMEM)] * count


def smem():
    return pl.BlockSpec(memory_space=pltpu.SMEM)


def pack_kernel(place, query_ref, key_ref, value_ref, q_own, q_other, kv_own, kv_other):
    half = place[0]
    for head, q_out, kv_out in ((half, q_own, kv_own), (1 - half, q_other, kv_other)):
        for part in range(2):
            at = pl.multiple_of(head * 256 + part * 128, 128)
            q_out[part * BLOCK : (part + 1) * BLOCK] = query_ref[:, pl.ds(at, 128)]
        at = pl.multiple_of(head * 128, 128)
        kv_out[:BLOCK] = key_ref[:, pl.ds(at, 128)]
        for part in range(4):
            rows = value_ref[part * 128 : (part + 1) * 128, pl.ds(at, 128)]
            kv_out[BLOCK + part * 128 : BLOCK + (part + 1) * 128] = (
                rows.astype(jnp.float32).T.astype(jnp.bfloat16)
            )


def keys_of(block):
    return block[:BLOCK]


def values_of(block):
    flipped = [block[BLOCK + part * 128 : BLOCK + (part + 1) * 128] for part in range(4)]
    ones = jnp.ones((EXT - HEAD_DIM, BLOCK), jnp.bfloat16)
    return jnp.concatenate([jnp.concatenate(flipped, axis=1), ones], axis=0)


def attend_kernel(place, q_ref, kv_ref, out_ref, best, acc):
    half, y, z = place[0], place[1], place[2]

    def scores(queries, keys):
        return lax.dot_general(keys, queries, CONTRACT_LAST, preferred_element_type=jnp.float32)

    def update(score, values):
        old = best[...]
        new = jnp.maximum(old, jnp.max(score, axis=0, keepdims=True))
        weights = jnp.exp2(score * SCALE - new * SCALE)
        rescale = jnp.exp2((old - new) * SCALE)
        best[...] = new
        acc[...] = acc[...] * rescale + jnp.dot(
            values, weights.astype(jnp.bfloat16), preferred_element_type=jnp.float32
        )

    def one_query_block(slot, _):
        q_half = jnp.where(slot < 4, half, 1 - half)
        q_row = 4 * q_half + lax.rem(y - lax.rem(slot, 4) + 4, 4)
        best[...] = jnp.full_like(best, LOWEST)
        acc[...] = jnp.zeros_like(acc)
        for which in range(2):
            own_row = 4 * half + y
            kv_row = own_row if which == 0 else 7 - own_row

            @pl.when(kv_row < q_row)
            def _():
                tiles = []
                for pair in range(2):
                    blocks = [kv_ref[4 * which + 2 * pair + part] for part in range(2)]
                    keys = jnp.concatenate([keys_of(b) for b in blocks], axis=0)
                    values = jnp.concatenate([values_of(b) for b in blocks], axis=1)
                    tiles.append((scores(q_ref[slot], keys), values))
                for score, values in tiles:
                    update(score, values)

            @pl.when(kv_row == q_row)
            def _():
                block = kv_ref[4 * which]
                score = scores(q_ref[slot], keys_of(block))
                key_at = lax.broadcasted_iota(jnp.int32, (BLOCK, ROWS), 0)
                token = lax.broadcasted_iota(jnp.int32, (BLOCK, ROWS), 1) & (BLOCK - 1)
                update(jnp.where(key_at <= token, score, LOWEST), values_of(block))
                for step in range(1, 4):

                    @pl.when(step <= z)
                    def _():
                        earlier = kv_ref[4 * which + step]
                        update(scores(q_ref[slot], keys_of(earlier)), values_of(earlier))

        total = acc[HEAD_DIM : HEAD_DIM + 1]
        empty = total == 0.0
        inverse = 1.0 / jnp.where(empty, 1.0, total)
        out_ref[slot, :HEAD_DIM] = (acc[:HEAD_DIM] * inverse).astype(jnp.bfloat16)
        level = best[...] * SCALE + jnp.log2(jnp.where(empty, 1.0, total))
        first = level.astype(jnp.bfloat16)
        rest = level - first.astype(jnp.float32)
        second = rest.astype(jnp.bfloat16)
        third = (rest - second.astype(jnp.float32)).astype(jnp.bfloat16)
        index = lax.broadcasted_iota(jnp.int32, (EXT - HEAD_DIM, ROWS), 0)
        rows = jnp.where(
            index == 0,
            first.astype(jnp.float32),
            jnp.where(index == 1, second.astype(jnp.float32), third.astype(jnp.float32)),
        )
        out_ref[slot, HEAD_DIM:] = rows.astype(jnp.bfloat16)
        return 0

    lax.fori_loop(0, 8, one_query_block, 0)


def merge_kernel(place, *refs):
    parts, out_ref = refs[:8], refs[8]
    half = place[0]
    for side in range(2):
        head = half if side == 0 else 1 - half
        group = parts[4 * side : 4 * side + 4]
        levels = []
        for part in group:
            tail = part[HEAD_DIM:].astype(jnp.float32)
            levels.append(tail[0:1] + tail[1:2] + tail[2:3])
        top = jnp.maximum(jnp.maximum(levels[0], levels[1]), jnp.maximum(levels[2], levels[3]))
        shares = [jnp.exp2(level - top) for level in levels]
        inverse = 1.0 / (shares[0] + shares[1] + shares[2] + shares[3])
        mixed = sum(
            part[:HEAD_DIM].astype(jnp.float32) * (share * inverse)
            for part, share in zip(group, shares)
        )
        for sub in range(2):
            at = pl.multiple_of(head * 256 + sub * 128, 128)
            out_ref[:, pl.ds(at, 128)] = mixed[:, sub * BLOCK : (sub + 1) * BLOCK].T.astype(
                jnp.bfloat16
            )


def ring(value, axis, steps):
    size = lax.axis_size(axis)
    return lax.ppermute(value, axis, [(at, (at + steps) % size) for at in range(size)])


def routed(value, target):
    pairs = []
    for half in range(2):
        for y in range(4):
            to_half, to_y = target(half, y)
            pairs.append((4 * half + y, 4 * to_half + to_y))
    return lax.ppermute(value, ("xl", "y"), pairs)


def on_device(query_rows, key_rows, value_rows):
    half, y, z = lax.axis_index("xl"), lax.axis_index("y"), lax.axis_index("z")
    place = jnp.stack([half, y, z]).astype(jnp.int32)
    message = jax.ShapeDtypeStruct((ROWS, 128), jnp.bfloat16)
    q_own, q_other, kv_own, kv_other = pl.pallas_call(
        pack_kernel,
        out_shape=(message,) * 4,
        in_specs=[smem()] + vmem(3),
        out_specs=tuple(vmem(4)),
        compiler_params=PARAMS,
    )(place, query_rows, key_rows, value_rows)
    kv_mirror = routed(kv_other, lambda h, r: (1 - h, 3 - r))
    q_swap = ring(q_other, "xl", 1)
    kv_all = jnp.stack(
        [kv_own] + [ring(kv_own, "z", k) for k in (1, 2, 3)]
        + [kv_mirror] + [ring(kv_mirror, "z", k) for k in (1, 2, 3)]
    )
    q_all = jnp.stack(
        [q_own] + [ring(q_own, "y", k) for k in (1, 2, 3)]
        + [q_swap] + [ring(q_swap, "y", k) for k in (1, 2, 3)]
    )
    partial = pl.pallas_call(
        attend_kernel,
        out_shape=jax.ShapeDtypeStruct((8, EXT, ROWS), jnp.bfloat16),
        in_specs=[smem()] + vmem(2),
        out_specs=vmem(1)[0],
        scratch_shapes=[pltpu.VMEM((1, ROWS), jnp.float32), pltpu.VMEM((EXT, ROWS), jnp.float32)],
        compiler_params=PARAMS,
    )(place, q_all, kv_all)
    parts = [partial[0]]
    parts += [ring(partial[k], "y", 4 - k) for k in (1, 2, 3)]
    parts += [
        routed(partial[4 + k], lambda h, r, k=k: (1 - h, (r - k) % 4)) for k in (0, 1, 2, 3)
    ]
    merged = pl.pallas_call(
        merge_kernel,
        out_shape=jax.ShapeDtypeStruct((BLOCK, 512), jnp.bfloat16),
        in_specs=[smem()] + vmem(8),
        out_specs=vmem(1)[0],
        compiler_params=PARAMS,
    )(place, *parts)
    return lax.all_to_all(merged, ("xh", "core"), split_axis=0, concat_axis=1, tiled=True)


def solution(mesh):
    fine = Mesh(mesh.devices.reshape(2, 4, 4, 2, 2), ("xl", "y", "z", "xh", "core"))
    tokens, heads = ("xl", "y", "z"), ("xh", "core")
    return jax.shard_map(
        on_device,
        mesh=fine,
        in_specs=(P(tokens, heads),) * 3,
        out_specs=P(tokens + heads, None),
        check_vma=False,
    )
```

```python
import functools

import jax
import jax.numpy as jnp
from jax import lax
from jax.experimental import pallas as pl
from jax.experimental.pallas import tpu as pltpu
from jax.sharding import Mesh, PartitionSpec as P

HEAD_DIM = 128
SCALAR = 168
SCALE = SCALAR ** (-0.5) * 1.4426950408889634
LOWEST = -1e30
BLOCK = 512
ROWS = 2 * BLOCK
EXT = HEAD_DIM + 16

CONTRACT_LAST = (((1,), (1,)), ((), ()))
PARAMS = pltpu.CompilerParams(vmem_limit_bytes=30 * 2**20)


def vmem(count):
    return [pl.BlockSpec(memory_space=pltpu.VMEM)] * count


def smem():
    return pl.BlockSpec(memory_space=pltpu.SMEM)


def pack_kernel(place, query_ref, key_ref, value_ref, q_own, q_other, kv_own, kv_other):
    half = place[0]
    for head, q_out, kv_out in ((half, q_own, kv_own), (1 - half, q_other, kv_other)):
        for part in range(2):
            at = pl.multiple_of(head * 256 + part * 128, 128)
            q_out[part * BLOCK : (part + 1) * BLOCK] = query_ref[:, pl.ds(at, 128)]
        at = pl.multiple_of(head * 128, 128)
        kv_out[:BLOCK] = key_ref[:, pl.ds(at, 128)]
        for part in range(4):
            rows = value_ref[part * 128 : (part + 1) * 128, pl.ds(at, 128)]
            kv_out[BLOCK + part * 128 : BLOCK + (part + 1) * 128] = (
                rows.astype(jnp.float32).T.astype(jnp.bfloat16)
            )


def keys_of(block):
    return block[:BLOCK]


def values_of(block):
    flipped = [block[BLOCK + part * 128 : BLOCK + (part + 1) * 128] for part in range(4)]
    ones = jnp.ones((EXT - HEAD_DIM, BLOCK), jnp.bfloat16)
    return jnp.concatenate([jnp.concatenate(flipped, axis=1), ones], axis=0)


def attend_kernel(step, place, q_ref, *refs):
    kv_refs, out_ref, best, acc = refs[:8], refs[8], refs[9], refs[10]
    half, y, z = place[0], place[1], place[2]

    def scores(queries, keys):
        return lax.dot_general(keys, queries, CONTRACT_LAST, preferred_element_type=jnp.float32)

    def update(score, values):
        old = best[...]
        new = jnp.maximum(old, jnp.max(score, axis=0, keepdims=True))
        weights = jnp.exp2(score * SCALE - new * SCALE)
        rescale = jnp.exp2((old - new) * SCALE)
        best[...] = new
        acc[...] = acc[...] * rescale + jnp.dot(
            values, weights.astype(jnp.bfloat16), preferred_element_type=jnp.float32
        )

    def one_query_block(slot, _):
        q_half = jnp.where(slot == 0, half, 1 - half)
        q_row = 4 * q_half + lax.rem(y - step + 4, 4)
        best[...] = jnp.full_like(best, LOWEST)
        acc[...] = jnp.zeros_like(acc)
        for which in range(2):
            own_row = 4 * half + y
            kv_row = own_row if which == 0 else 7 - own_row
            row_refs = kv_refs[4 * which : 4 * which + 4]

            @pl.when(kv_row < q_row)
            def _():
                tiles = []
                for pair in range(2):
                    blocks = [row_refs[2 * pair + part][...] for part in range(2)]
                    keys = jnp.concatenate([keys_of(b) for b in blocks], axis=0)
                    values = jnp.concatenate([values_of(b) for b in blocks], axis=1)
                    tiles.append((scores(q_ref[slot], keys), values))
                for score, values in tiles:
                    update(score, values)

            @pl.when(kv_row == q_row)
            def _():
                block = row_refs[0][...]
                score = scores(q_ref[slot], keys_of(block))
                key_at = lax.broadcasted_iota(jnp.int32, (BLOCK, ROWS), 0)
                token = lax.broadcasted_iota(jnp.int32, (BLOCK, ROWS), 1) & (BLOCK - 1)
                update(jnp.where(key_at <= token, score, LOWEST), values_of(block))
                for back in range(1, 4):

                    @pl.when(back <= z)
                    def _():
                        earlier = row_refs[back][...]
                        update(scores(q_ref[slot], keys_of(earlier)), values_of(earlier))

        total = acc[HEAD_DIM : HEAD_DIM + 1]
        empty = total == 0.0
        inverse = 1.0 / jnp.where(empty, 1.0, total)
        out_ref[slot, :HEAD_DIM] = (acc[:HEAD_DIM] * inverse).astype(jnp.bfloat16)
        level = best[...] * SCALE + jnp.log2(jnp.where(empty, 1.0, total))
        first = level.astype(jnp.bfloat16)
        rest = level - first.astype(jnp.float32)
        second = rest.astype(jnp.bfloat16)
        third = (rest - second.astype(jnp.float32)).astype(jnp.bfloat16)
        index = lax.broadcasted_iota(jnp.int32, (EXT - HEAD_DIM, ROWS), 0)
        rows = jnp.where(
            index == 0,
            first.astype(jnp.float32),
            jnp.where(index == 1, second.astype(jnp.float32), third.astype(jnp.float32)),
        )
        out_ref[slot, HEAD_DIM:] = rows.astype(jnp.bfloat16)
        return 0

    lax.fori_loop(0, 2, one_query_block, 0)


def attend(step, place, queries, blocks):
    return pl.pallas_call(
        functools.partial(attend_kernel, step),
        out_shape=jax.ShapeDtypeStruct((2, EXT, ROWS), jnp.bfloat16),
        in_specs=[smem()] + vmem(9),
        out_specs=vmem(1)[0],
        scratch_shapes=[pltpu.VMEM((1, ROWS), jnp.float32), pltpu.VMEM((EXT, ROWS), jnp.float32)],
        compiler_params=PARAMS,
        name=f"attend{step}",
    )(place, queries, *blocks)


def merge_kernel(place, *refs):
    parts, out_ref = refs[:4], refs[4]
    half = place[0]
    for slot in range(2):
        levels = []
        for part in parts:
            tail = part[slot, HEAD_DIM:].astype(jnp.float32)
            levels.append(tail[0:1] + tail[1:2] + tail[2:3])
        top = jnp.maximum(jnp.maximum(levels[0], levels[1]), jnp.maximum(levels[2], levels[3]))
        shares = [jnp.exp2(level - top) for level in levels]
        inverse = 1.0 / (shares[0] + shares[1] + shares[2] + shares[3])
        mixed = sum(
            part[slot, :HEAD_DIM].astype(jnp.float32) * (share * inverse)
            for part, share in zip(parts, shares)
        )
        row_half = half if slot == 0 else 1 - half
        for sub in range(2):
            for piece in range(4):
                at = sub * BLOCK + piece * 128
                out_ref[piece, row_half, :, sub * 128 : (sub + 1) * 128] = (
                    mixed[:, at : at + 128].T.astype(jnp.bfloat16)
                )


def ring(value, axis, steps):
    size = lax.axis_size(axis)
    return lax.ppermute(value, axis, [(at, (at + steps) % size) for at in range(size)])


def routed(value, target):
    pairs = []
    for half in range(2):
        for y in range(4):
            to_half, to_y = target(half, y)
            pairs.append((4 * half + y, 4 * to_half + to_y))
    return lax.ppermute(value, ("xl", "y"), pairs)


def on_device(query_rows, key_rows, value_rows):
    half, y, z = lax.axis_index("xl"), lax.axis_index("y"), lax.axis_index("z")
    place = jnp.stack([half, y, z]).astype(jnp.int32)
    message = jax.ShapeDtypeStruct((ROWS, 128), jnp.bfloat16)
    q_own, q_other, kv_own, kv_other = pl.pallas_call(
        pack_kernel,
        out_shape=(message,) * 4,
        in_specs=[smem()] + vmem(3),
        out_specs=tuple(vmem(4)),
        compiler_params=PARAMS,
    )(place, query_rows, key_rows, value_rows)
    kv_mirror = routed(kv_other, lambda h, r: (1 - h, 3 - r))
    q_swap = ring(q_other, "xl", 1)
    blocks = [kv_own] + [ring(kv_own, "z", k) for k in (1, 2, 3)]
    blocks += [kv_mirror] + [ring(kv_mirror, "z", k) for k in (1, 2, 3)]
    queries = [jnp.stack([q_own, q_swap])]
    queries += [jnp.stack([ring(q_own, "y", k), ring(q_swap, "y", k)]) for k in (1, 2, 3)]
    parts = [ring(attend(k, place, queries[k], blocks), "y", 4 - k) for k in (1, 3, 2)]
    parts.append(attend(0, place, queries[0], blocks))
    merged = pl.pallas_call(
        merge_kernel,
        out_shape=jax.ShapeDtypeStruct((4, 2, 128, 256), jnp.bfloat16),
        in_specs=[smem()] + vmem(4),
        out_specs=vmem(1)[0],
        compiler_params=PARAMS,
        name="merge",
    )(place, *parts)
    merged = merged.reshape(8, 128, 256)
    spread = lax.all_to_all(merged, ("xh", "core", "xl"), split_axis=0, concat_axis=0, tiled=True)
    return spread.transpose(1, 0, 2).reshape(128, 2048)


def solution(mesh):
    fine = Mesh(mesh.devices.reshape(2, 4, 4, 2, 2), ("xl", "y", "z", "xh", "core"))
    tokens, heads = ("xl", "y", "z"), ("xh", "core")
    return jax.shard_map(
        on_device,
        mesh=fine,
        in_specs=(P(tokens, heads),) * 3,
        out_specs=P(tokens + heads, None),
        check_vma=False,
    )
```

```python
import functools

import jax
import jax.numpy as jnp
from jax import lax
from jax.experimental import pallas as pl
from jax.experimental.pallas import tpu as pltpu
from jax.sharding import Mesh, PartitionSpec as P

HEAD_DIM = 128
SCALAR = 168
SCALE = SCALAR ** (-0.5) * 1.4426950408889634
LOWEST = -1e30
BLOCK = 512
ROWS = 2 * BLOCK
EXT = HEAD_DIM + 16
STRIP = 256
STRIPS = ROWS // STRIP

CONTRACT_LAST = (((1,), (1,)), ((), ()))
PARAMS = pltpu.CompilerParams(vmem_limit_bytes=30 * 2**20)


def vmem(count):
    return [pl.BlockSpec(memory_space=pltpu.VMEM)] * count


def smem():
    return pl.BlockSpec(memory_space=pltpu.SMEM)


def pack_keys_kernel(place, key_ref, value_ref, kv_own, kv_other):
    half = place[0]
    for head, kv_out in ((1 - half, kv_other), (half, kv_own)):
        at = pl.multiple_of(head * 128, 128)
        kv_out[:BLOCK] = key_ref[:, pl.ds(at, 128)]
        for part in range(4):
            rows = value_ref[part * 128 : (part + 1) * 128, pl.ds(at, 128)]
            kv_out[BLOCK + part * 128 : BLOCK + (part + 1) * 128] = (
                rows.astype(jnp.float32).T.astype(jnp.bfloat16)
            )


def pack_queries_kernel(place, query_ref, after, q_own, q_other):
    half = place[0]
    for head, q_out in ((1 - half, q_other), (half, q_own)):
        for part in range(2):
            at = pl.multiple_of(head * 256 + part * 128, 128)
            q_out[part * BLOCK : (part + 1) * BLOCK] = query_ref[:, pl.ds(at, 128)]


def whole(shape):
    return pl.BlockSpec(shape, lambda _: (0,) * len(shape))


def attend_kernel(step, place, q_ref, kv_ref, out_ref, best, acc, held, peak, todo):
    half, y, z = place[0], place[1], place[2]
    own_row = 4 * half + y
    kv_rows = (own_row, 7 - own_row)
    back = lax.rem(y - step + 4, 4)
    q_rows = (4 * half + back, 4 * (1 - half) + back)

    def keys_of(tile):
        _, row, pair = tile
        at = 4 * row + 2 * pair
        return jnp.concatenate([kv_ref[at + part, :BLOCK] for part in range(2)], axis=0)

    def values_of(tile):
        _, row, pair = tile
        at = 4 * row + 2 * pair
        flipped = [
            kv_ref[at + part, BLOCK + piece * 128 : BLOCK + (piece + 1) * 128]
            for part in range(2)
            for piece in range(4)
        ]
        ones = jnp.ones((EXT - HEAD_DIM, 2 * BLOCK), jnp.bfloat16)
        return jnp.concatenate([jnp.concatenate(flipped, axis=1), ones], axis=0)

    def score(tile, keys, strip, mask=None):
        part = lax.dot_general(
            keys,
            q_ref[tile[0], strip * STRIP : (strip + 1) * STRIP],
            CONTRACT_LAST,
            preferred_element_type=jnp.float32,
        )
        if mask is not None:
            part = mask(part, strip)
        held[strip] = part
        peak[strip] = jnp.max(part, axis=0, keepdims=True)

    def update(tile, values, strip):
        slot = tile[0]
        old = best[slot, strip]
        new = jnp.maximum(old, peak[strip])
        weights = jnp.exp2(held[strip] * SCALE - new * SCALE)
        rescale = jnp.exp2((old - new) * SCALE)
        best[slot, strip] = new
        acc[slot, strip] = acc[slot, strip] * rescale + jnp.dot(
            values, weights.astype(jnp.bfloat16), preferred_element_type=jnp.float32
        )

    best[...] = jnp.full_like(best, LOWEST)
    acc[...] = jnp.zeros_like(acc)
    todo[0] = 0
    for slot in range(2):
        for row in range(2):

            @pl.when(kv_rows[row] < q_rows[slot])
            def _():
                count = todo[0]
                todo[1 + count] = 2 * slot + row
                todo[0] = count + 1

    def tile_at(at):
        entry = todo[1 + at // 2]
        return entry // 2, entry % 2, at % 2

    count = 2 * todo[0]

    @pl.when(count > 0)
    def _():
        start = tile_at(0)
        keys = keys_of(start)
        for strip in range(STRIPS):
            score(start, keys, strip)

        def step_on(at):
            now, later = tile_at(at), tile_at(at + 1)
            values, keys = values_of(now), keys_of(later)
            for strip in range(STRIPS):
                update(now, values, strip)
                score(later, keys, strip)

        def one(at, _):
            step_on(2 * at)
            step_on(2 * at + 1)
            return 0

        lax.fori_loop(0, todo[0] - 1, one, 0)
        step_on(count - 2)
        last = tile_at(count - 1)
        values = values_of(last)
        for strip in range(STRIPS):
            update(last, values, strip)

    def on_the_diagonal(slot, row):
        def causal(part, strip):
            key_at = lax.broadcasted_iota(jnp.int32, (BLOCK, STRIP), 0)
            token = lax.broadcasted_iota(jnp.int32, (BLOCK, STRIP), 1) + strip * STRIP % BLOCK
            near = jnp.where(key_at <= token, part[:BLOCK], LOWEST)
            return jnp.concatenate([near, jnp.where(z >= 1, part[BLOCK:], LOWEST)], axis=0)

        def far(part, strip):
            return jnp.concatenate(
                [part[:BLOCK], jnp.where(z >= 3, part[BLOCK:], LOWEST)], axis=0
            )

        def alone(pair, mask):
            tile = (slot, row, pair)
            keys, values = keys_of(tile), values_of(tile)
            for strip in range(STRIPS):
                score(tile, keys, strip, mask)
            for strip in range(STRIPS):
                update(tile, values, strip)

        alone(0, causal)
        pl.when(z >= 2)(lambda: alone(1, far))

    if step == 0:
        on_the_diagonal(0, 0)
    if step % 2 == 1:
        pl.when(kv_rows[1] == q_rows[1])(lambda: on_the_diagonal(1, 1))

    index = lax.broadcasted_iota(jnp.int32, (EXT - HEAD_DIM, STRIP), 0)
    for slot in range(2):
        for strip in range(STRIPS):
            at = slice(strip * STRIP, (strip + 1) * STRIP)
            total = acc[slot, strip, HEAD_DIM : HEAD_DIM + 1]
            empty = total == 0.0
            inverse = 1.0 / jnp.where(empty, 1.0, total)
            out_ref[slot, :HEAD_DIM, at] = (acc[slot, strip, :HEAD_DIM] * inverse).astype(
                jnp.bfloat16
            )
            level = best[slot, strip] * SCALE + jnp.log2(jnp.where(empty, 1.0, total))
            high = level.astype(jnp.bfloat16).astype(jnp.float32)
            middle = (level - high).astype(jnp.bfloat16).astype(jnp.float32)
            low = level - high - middle
            rows = jnp.where(index == 0, high, jnp.where(index == 1, middle, low))
            out_ref[slot, HEAD_DIM:, at] = rows.astype(jnp.bfloat16)


def attend(step, place, queries, blocks):
    return pl.pallas_call(
        functools.partial(attend_kernel, step),
        out_shape=jax.ShapeDtypeStruct((2, EXT, ROWS), jnp.bfloat16),
        in_specs=[smem()] + vmem(2),
        out_specs=vmem(1)[0],
        scratch_shapes=[
            pltpu.VMEM((2, STRIPS, 1, STRIP), jnp.float32),
            pltpu.VMEM((2, STRIPS, EXT, STRIP), jnp.float32),
            pltpu.VMEM((STRIPS, 2 * BLOCK, STRIP), jnp.float32),
            pltpu.VMEM((STRIPS, 1, STRIP), jnp.float32),
            pltpu.SMEM((8,), jnp.int32),
        ],
        compiler_params=PARAMS,
        name=f"attend{step}",
    )(place, queries, blocks)


def merge_kernel(place, *refs):
    parts, out_ref = refs[:4], refs[4]
    half = place[0]
    for slot in range(2):
        levels = []
        for part in parts:
            tail = part[slot, HEAD_DIM:].astype(jnp.float32)
            levels.append(tail[0:1] + tail[1:2] + tail[2:3])
        top = jnp.maximum(jnp.maximum(levels[0], levels[1]), jnp.maximum(levels[2], levels[3]))
        shares = [jnp.exp2(level - top) for level in levels]
        inverse = 1.0 / (shares[0] + shares[1] + shares[2] + shares[3])
        mixed = sum(
            part[slot, :HEAD_DIM].astype(jnp.float32) * (share * inverse)
            for part, share in zip(parts, shares)
        )
        row_half = half if slot == 0 else 1 - half
        for sub in range(2):
            for piece in range(4):
                at = sub * BLOCK + piece * 128
                out_ref[piece, row_half, :, sub * 128 : (sub + 1) * 128] = (
                    mixed[:, at : at + 128].T.astype(jnp.bfloat16)
                )


def ring(value, axis, steps):
    size = lax.axis_size(axis)
    return lax.ppermute(value, axis, [(at, (at + steps) % size) for at in range(size)])


def routed(value, target):
    pairs = []
    for half in range(2):
        for y in range(4):
            to_half, to_y = target(half, y)
            pairs.append((4 * half + y, 4 * to_half + to_y))
    return lax.ppermute(value, ("xl", "y"), pairs)


def on_device(query_rows, key_rows, value_rows):
    half, y, z = lax.axis_index("xl"), lax.axis_index("y"), lax.axis_index("z")
    place = jnp.stack([half, y, z]).astype(jnp.int32)
    message = jax.ShapeDtypeStruct((ROWS, 128), jnp.bfloat16)
    kv_own, kv_other = pl.pallas_call(
        pack_keys_kernel,
        grid=(1,),
        out_shape=(message,) * 2,
        in_specs=[smem(), whole((BLOCK, 256)), whole((BLOCK, 256))],
        out_specs=tuple(vmem(2)),
        compiler_params=PARAMS,
        name="pack_keys",
    )(place, key_rows, value_rows)
    q_own, q_other = pl.pallas_call(
        pack_queries_kernel,
        grid=(1,),
        out_shape=(message,) * 2,
        in_specs=[smem(), whole((BLOCK, 512)), pl.BlockSpec(memory_space=pl.ANY)],
        out_specs=tuple(vmem(2)),
        compiler_params=PARAMS,
        name="pack_queries",
    )(place, query_rows, kv_own)
    kv_mirror = routed(kv_other, lambda h, r: (1 - h, 3 - r))
    q_swap = ring(q_other, "xl", 1)
    blocks = [kv_own] + [ring(kv_own, "z", k) for k in (1, 2, 3)]
    blocks += [kv_mirror] + [ring(kv_mirror, "z", k) for k in (1, 2, 3)]
    blocks = jnp.stack(blocks)
    queries = [jnp.stack([q_own, q_swap])]
    queries += [jnp.stack([ring(q_own, "y", k), ring(q_swap, "y", k)]) for k in (1, 2, 3)]
    parts = [ring(attend(k, place, queries[k], blocks), "y", 4 - k) for k in (1, 3, 2)]
    parts.append(attend(0, place, queries[0], blocks))
    merged = pl.pallas_call(
        merge_kernel,
        out_shape=jax.ShapeDtypeStruct((4, 2, 128, 256), jnp.bfloat16),
        in_specs=[smem()] + vmem(4),
        out_specs=vmem(1)[0],
        compiler_params=PARAMS,
        name="merge",
    )(place, *parts)
    merged = merged.reshape(8, 128, 256)
    spread = lax.all_to_all(merged, ("xh", "core", "xl"), split_axis=0, concat_axis=0, tiled=True)
    return spread.transpose(1, 0, 2).reshape(128, 2048)


def solution(mesh):
    fine = Mesh(mesh.devices.reshape(2, 4, 4, 2, 2), ("xl", "y", "z", "xh", "core"))
    tokens, heads = ("xl", "y", "z"), ("xh", "core")
    return jax.shard_map(
        on_device,
        mesh=fine,
        in_specs=(P(tokens, heads),) * 3,
        out_specs=P(tokens + heads, None),
        check_vma=False,
    )
```

```python
import functools

import jax
import jax.numpy as jnp
from jax import lax
from jax.experimental import pallas as pl
from jax.experimental.pallas import tpu as pltpu
from jax.sharding import Mesh, PartitionSpec as P

HEAD_DIM = 128
SCALAR = 168
SCALE = SCALAR ** (-0.5) * 1.4426950408889634
LOWEST = -1e30
BLOCK = 512
ROWS = 2 * BLOCK
EXT = HEAD_DIM + 16
STRIP = 256
STRIPS = ROWS // STRIP

CONTRACT_LAST = (((1,), (1,)), ((), ()))
PARAMS = pltpu.CompilerParams(vmem_limit_bytes=30 * 2**20)


def vmem(count):
    return [pl.BlockSpec(memory_space=pltpu.VMEM)] * count


def smem():
    return pl.BlockSpec(memory_space=pltpu.SMEM)


def pack_keys_kernel(place, key_in, value_in, kv_own, kv_other, key_ref, value_ref, done):
    half = place[0]
    keys = pltpu.make_async_copy(key_in, key_ref, done.at[0])
    values = pltpu.make_async_copy(value_in, value_ref, done.at[1])
    keys.start()
    values.start()
    keys.wait()
    values.wait()
    for head, kv_out in ((1 - half, kv_other), (half, kv_own)):
        at = pl.multiple_of(head * 128, 128)
        kv_out[:BLOCK] = key_ref[:, pl.ds(at, 128)]
        for part in range(4):
            rows = value_ref[part * 128 : (part + 1) * 128, pl.ds(at, 128)]
            kv_out[BLOCK + part * 128 : BLOCK + (part + 1) * 128] = (
                rows.astype(jnp.float32).T.astype(jnp.bfloat16)
            )


def pack_queries_kernel(place, query_in, after, q_own, q_other, query_ref, done):
    half = place[0]
    queries = pltpu.make_async_copy(query_in, query_ref, done)
    queries.start()
    queries.wait()
    for head, q_out in ((1 - half, q_other), (half, q_own)):
        for part in range(2):
            at = pl.multiple_of(head * 256 + part * 128, 128)
            q_out[part * BLOCK : (part + 1) * BLOCK] = query_ref[:, pl.ds(at, 128)]


def attend_kernel(step, place, q_ref, kv_ref, out_ref, best, acc, held, peak, todo):
    half, y, z = place[0], place[1], place[2]
    own_row = 4 * half + y
    kv_rows = (own_row, 7 - own_row)
    back = lax.rem(y - step + 4, 4)
    q_rows = (4 * half + back, 4 * (1 - half) + back)

    def keys_of(tile):
        _, row, pair = tile
        at = 4 * row + 2 * pair
        return jnp.concatenate([kv_ref[at + part, :BLOCK] for part in range(2)], axis=0)

    def values_of(tile):
        _, row, pair = tile
        at = 4 * row + 2 * pair
        flipped = [
            kv_ref[at + part, BLOCK + piece * 128 : BLOCK + (piece + 1) * 128]
            for part in range(2)
            for piece in range(4)
        ]
        ones = jnp.ones((EXT - HEAD_DIM, 2 * BLOCK), jnp.bfloat16)
        return jnp.concatenate([jnp.concatenate(flipped, axis=1), ones], axis=0)

    def score(tile, keys, strip, mask=None):
        part = lax.dot_general(
            keys,
            q_ref[tile[0], strip * STRIP : (strip + 1) * STRIP],
            CONTRACT_LAST,
            preferred_element_type=jnp.float32,
        )
        if mask is not None:
            part = mask(part, strip)
        held[strip] = part
        peak[strip] = jnp.max(part, axis=0, keepdims=True)

    def update(tile, values, strip):
        slot = tile[0]
        old = best[slot, strip]
        new = jnp.maximum(old, peak[strip])
        weights = jnp.exp2(held[strip] * SCALE - new * SCALE)
        rescale = jnp.exp2((old - new) * SCALE)
        best[slot, strip] = new
        acc[slot, strip] = acc[slot, strip] * rescale + jnp.dot(
            values, weights.astype(jnp.bfloat16), preferred_element_type=jnp.float32
        )

    best[...] = jnp.full_like(best, LOWEST)
    acc[...] = jnp.zeros_like(acc)
    todo[0] = 0
    for slot in range(2):
        for row in range(2):

            @pl.when(kv_rows[row] < q_rows[slot])
            def _():
                count = todo[0]
                todo[1 + count] = 2 * slot + row
                todo[0] = count + 1

    def tile_at(at):
        entry = todo[1 + at // 2]
        return entry // 2, entry % 2, at % 2

    count = 2 * todo[0]

    @pl.when(count > 0)
    def _():
        start = tile_at(0)
        keys = keys_of(start)
        for strip in range(STRIPS):
            score(start, keys, strip)

        def step_on(at):
            now, later = tile_at(at), tile_at(at + 1)
            values, keys = values_of(now), keys_of(later)
            for strip in range(STRIPS):
                update(now, values, strip)
                score(later, keys, strip)

        def one(at, _):
            step_on(2 * at)
            step_on(2 * at + 1)
            return 0

        lax.fori_loop(0, todo[0] - 1, one, 0)
        step_on(count - 2)
        last = tile_at(count - 1)
        values = values_of(last)
        for strip in range(STRIPS):
            update(last, values, strip)

    def on_the_diagonal(slot, row):
        def causal(part, strip):
            key_at = lax.broadcasted_iota(jnp.int32, (BLOCK, STRIP), 0)
            token = lax.broadcasted_iota(jnp.int32, (BLOCK, STRIP), 1) + strip * STRIP % BLOCK
            near = jnp.where(key_at <= token, part[:BLOCK], LOWEST)
            return jnp.concatenate([near, jnp.where(z >= 1, part[BLOCK:], LOWEST)], axis=0)

        def far(part, strip):
            return jnp.concatenate(
                [part[:BLOCK], jnp.where(z >= 3, part[BLOCK:], LOWEST)], axis=0
            )

        def alone(pair, mask):
            tile = (slot, row, pair)
            keys, values = keys_of(tile), values_of(tile)
            for strip in range(STRIPS):
                score(tile, keys, strip, mask)
            for strip in range(STRIPS):
                update(tile, values, strip)

        alone(0, causal)
        pl.when(z >= 2)(lambda: alone(1, far))

    if step == 0:
        on_the_diagonal(0, 0)
    if step % 2 == 1:
        pl.when(kv_rows[1] == q_rows[1])(lambda: on_the_diagonal(1, 1))

    index = lax.broadcasted_iota(jnp.int32, (EXT - HEAD_DIM, STRIP), 0)
    for slot in range(2):
        for strip in range(STRIPS):
            at = slice(strip * STRIP, (strip + 1) * STRIP)
            total = acc[slot, strip, HEAD_DIM : HEAD_DIM + 1]
            empty = total == 0.0
            inverse = 1.0 / jnp.where(empty, 1.0, total)
            out_ref[slot, :HEAD_DIM, at] = (acc[slot, strip, :HEAD_DIM] * inverse).astype(
                jnp.bfloat16
            )
            level = best[slot, strip] * SCALE + jnp.log2(jnp.where(empty, 1.0, total))
            high = level.astype(jnp.bfloat16).astype(jnp.float32)
            middle = (level - high).astype(jnp.bfloat16).astype(jnp.float32)
            low = level - high - middle
            rows = jnp.where(index == 0, high, jnp.where(index == 1, middle, low))
            out_ref[slot, HEAD_DIM:, at] = rows.astype(jnp.bfloat16)


def attend(step, place, queries, blocks):
    return pl.pallas_call(
        functools.partial(attend_kernel, step),
        out_shape=jax.ShapeDtypeStruct((2, EXT, ROWS), jnp.bfloat16),
        in_specs=[smem()] + vmem(2),
        out_specs=vmem(1)[0],
        scratch_shapes=[
            pltpu.VMEM((2, STRIPS, 1, STRIP), jnp.float32),
            pltpu.VMEM((2, STRIPS, EXT, STRIP), jnp.float32),
            pltpu.VMEM((STRIPS, 2 * BLOCK, STRIP), jnp.float32),
            pltpu.VMEM((STRIPS, 1, STRIP), jnp.float32),
            pltpu.SMEM((8,), jnp.int32),
        ],
        compiler_params=PARAMS,
        name=f"attend{step}",
    )(place, queries, blocks)


def merge_kernel(place, *refs):
    parts, out_ref = refs[:4], refs[4]
    half = place[0]
    for slot in range(2):
        levels = []
        for part in parts:
            tail = part[slot, HEAD_DIM:].astype(jnp.float32)
            levels.append(tail[0:1] + tail[1:2] + tail[2:3])
        top = jnp.maximum(jnp.maximum(levels[0], levels[1]), jnp.maximum(levels[2], levels[3]))
        shares = [jnp.exp2(level - top) for level in levels]
        inverse = 1.0 / (shares[0] + shares[1] + shares[2] + shares[3])
        mixed = sum(
            part[slot, :HEAD_DIM].astype(jnp.float32) * (share * inverse)
            for part, share in zip(parts, shares)
        )
        row_half = half if slot == 0 else 1 - half
        for sub in range(2):
            for piece in range(4):
                at = sub * BLOCK + piece * 128
                out_ref[piece, row_half, :, sub * 128 : (sub + 1) * 128] = (
                    mixed[:, at : at + 128].T.astype(jnp.bfloat16)
                )


def ring(value, axis, steps):
    size = lax.axis_size(axis)
    return lax.ppermute(value, axis, [(at, (at + steps) % size) for at in range(size)])


def routed(value, target):
    pairs = []
    for half in range(2):
        for y in range(4):
            to_half, to_y = target(half, y)
            pairs.append((4 * half + y, 4 * to_half + to_y))
    return lax.ppermute(value, ("xl", "y"), pairs)


def on_device(query_rows, key_rows, value_rows):
    half, y, z = lax.axis_index("xl"), lax.axis_index("y"), lax.axis_index("z")
    place = jnp.stack([half, y, z]).astype(jnp.int32)
    message = jax.ShapeDtypeStruct((ROWS, 128), jnp.bfloat16)
    kv_own, kv_other = pl.pallas_call(
        pack_keys_kernel,
        out_shape=(message,) * 2,
        in_specs=[smem()] + [pl.BlockSpec(memory_space=pltpu.HBM), pl.BlockSpec(memory_space=pltpu.HBM)],
        out_specs=tuple(vmem(2)),
        scratch_shapes=[
            pltpu.VMEM((BLOCK, 256), jnp.bfloat16),
            pltpu.VMEM((BLOCK, 256), jnp.bfloat16),
            pltpu.SemaphoreType.DMA((2,)),
        ],
        compiler_params=PARAMS,
        name="pack_keys",
    )(place, key_rows, value_rows)
    q_own, q_other = pl.pallas_call(
        pack_queries_kernel,
        out_shape=(message,) * 2,
        in_specs=[smem()] + [pl.BlockSpec(memory_space=pltpu.HBM), pl.BlockSpec(memory_space=pl.ANY)],
        out_specs=tuple(vmem(2)),
        scratch_shapes=[pltpu.VMEM((BLOCK, 512), jnp.bfloat16), pltpu.SemaphoreType.DMA],
        compiler_params=PARAMS,
        name="pack_queries",
    )(place, query_rows, kv_own)
    kv_mirror = routed(kv_other, lambda h, r: (1 - h, 3 - r))
    q_swap = ring(q_other, "xl", 1)
    kv_own, _ = lax.optimization_barrier((kv_own, q_other))
    own_near = [ring(kv_own, "z", k) for k in (1, 3)]
    mirror_near = [ring(kv_mirror, "z", k) for k in (1, 3)]
    kv_far = ring(jnp.stack([kv_own, kv_mirror]), "z", 2)
    blocks = jnp.stack(
        [kv_own, own_near[0], kv_far[0], own_near[1]]
        + [kv_mirror, mirror_near[0], kv_far[1], mirror_near[1]]
    )
    q_pair = jnp.stack([q_own, q_swap])
    queries = {k: ring(q_pair, "y", k) for k in (1, 3)}
    q_late, _ = lax.optimization_barrier((q_pair, mirror_near[1]))
    queries[2] = ring(q_late, "y", 2)
    queries[0] = q_pair
    parts = [ring(attend(k, place, queries[k], blocks), "y", 4 - k) for k in (1, 3, 2)]
    parts.append(attend(0, place, queries[0], blocks))
    merged = pl.pallas_call(
        merge_kernel,
        out_shape=jax.ShapeDtypeStruct((4, 2, 128, 256), jnp.bfloat16),
        in_specs=[smem()] + vmem(4),
        out_specs=vmem(1)[0],
        compiler_params=PARAMS,
        name="merge",
    )(place, *parts)
    merged = merged.reshape(8, 128, 256)
    spread = lax.all_to_all(merged, ("xh", "core", "xl"), split_axis=0, concat_axis=0, tiled=True)
    return spread.transpose(1, 0, 2).reshape(128, 2048)


def solution(mesh):
    fine = Mesh(mesh.devices.reshape(2, 4, 4, 2, 2), ("xl", "y", "z", "xh", "core"))
    tokens, heads = ("xl", "y", "z"), ("xh", "core")
    return jax.shard_map(
        on_device,
        mesh=fine,
        in_specs=(P(tokens, heads),) * 3,
        out_specs=P(tokens + heads, None),
        check_vma=False,
    )
```

```python
import functools

import jax
import jax.numpy as jnp
from jax import lax
from jax.experimental import pallas as pl
from jax.experimental.pallas import tpu as pltpu
from jax.sharding import Mesh, PartitionSpec as P

HEAD_DIM = 128
SCALAR = 168
SCALE = SCALAR ** (-0.5) * 1.4426950408889634
LOWEST = -1e30
BLOCK = 512
ROWS = 2 * BLOCK
EXT = HEAD_DIM + 16
STRIP = 256
STRIPS = ROWS // STRIP

CONTRACT_LAST = (((1,), (1,)), ((), ()))
PARAMS = pltpu.CompilerParams(vmem_limit_bytes=30 * 2**20)


def vmem(count):
    return [pl.BlockSpec(memory_space=pltpu.VMEM)] * count


def smem():
    return pl.BlockSpec(memory_space=pltpu.SMEM)


def pack_keys_kernel(place, key_in, value_in, kv_own, kv_other, key_ref, value_ref, done):
    half = place[0]
    keys = pltpu.make_async_copy(key_in, key_ref, done.at[0])
    values = pltpu.make_async_copy(value_in, value_ref, done.at[1])
    keys.start()
    values.start()
    keys.wait()
    values.wait()
    for head, kv_out in ((1 - half, kv_other), (half, kv_own)):
        at = pl.multiple_of(head * 128, 128)
        kv_out[:BLOCK] = key_ref[:, pl.ds(at, 128)]
        for part in range(4):
            rows = value_ref[part * 128 : (part + 1) * 128, pl.ds(at, 128)]
            kv_out[BLOCK + part * 128 : BLOCK + (part + 1) * 128] = (
                rows.astype(jnp.float32).T.astype(jnp.bfloat16)
            )


def pack_queries_kernel(place, query_in, after, q_own, q_other, query_ref, done):
    half = place[0]
    queries = pltpu.make_async_copy(query_in, query_ref, done)
    queries.start()
    queries.wait()
    for head, q_out in ((1 - half, q_other), (half, q_own)):
        for part in range(2):
            at = pl.multiple_of(head * 256 + part * 128, 128)
            q_out[part * BLOCK : (part + 1) * BLOCK] = query_ref[:, pl.ds(at, 128)]


def attend_kernel(step, place, q_ref, kv_ref, out_ref, best, acc, held, peak, todo):
    half, y, z = place[0], place[1], place[2]
    own_row = 4 * half + y
    kv_rows = (own_row, 7 - own_row)
    back = lax.rem(y - step + 4, 4)
    q_rows = (4 * half + back, 4 * (1 - half) + back)

    def keys_of(tile):
        _, row, pair = tile
        at = 4 * row + 2 * pair
        return jnp.concatenate([kv_ref[at + part, :BLOCK] for part in range(2)], axis=0)

    def values_of(tile):
        _, row, pair = tile
        at = 4 * row + 2 * pair
        flipped = [
            kv_ref[at + part, BLOCK + piece * 128 : BLOCK + (piece + 1) * 128]
            for part in range(2)
            for piece in range(4)
        ]
        ones = jnp.ones((EXT - HEAD_DIM, 2 * BLOCK), jnp.bfloat16)
        return jnp.concatenate([jnp.concatenate(flipped, axis=1), ones], axis=0)

    def score(tile, keys, strip, mask=None):
        part = lax.dot_general(
            keys,
            q_ref[tile[0], strip * STRIP : (strip + 1) * STRIP],
            CONTRACT_LAST,
            preferred_element_type=jnp.float32,
        )
        if mask is not None:
            part = mask(part, strip)
        held[strip] = part
        peak[strip] = jnp.max(part, axis=0, keepdims=True)

    def update(tile, values, strip):
        slot = tile[0]
        old = best[slot, strip]
        new = jnp.maximum(old, peak[strip])
        weights = jnp.exp2(held[strip] * SCALE - new * SCALE)
        rescale = jnp.exp2((old - new) * SCALE)
        best[slot, strip] = new
        acc[slot, strip] = acc[slot, strip] * rescale + jnp.dot(
            values, weights.astype(jnp.bfloat16), preferred_element_type=jnp.float32
        )

    best[...] = jnp.full_like(best, LOWEST)
    acc[...] = jnp.zeros_like(acc)
    todo[0] = 0
    for slot in range(2):
        for row in range(2):

            @pl.when(kv_rows[row] < q_rows[slot])
            def _():
                count = todo[0]
                todo[1 + count] = 2 * slot + row
                todo[0] = count + 1

    def tile_at(at):
        entry = todo[1 + at // 2]
        return entry // 2, entry % 2, at % 2

    count = 2 * todo[0]

    @pl.when(count > 0)
    def _():
        start = tile_at(0)
        keys = keys_of(start)
        for strip in range(STRIPS):
            score(start, keys, strip)

        def step_on(at):
            now, later = tile_at(at), tile_at(at + 1)
            values, keys = values_of(now), keys_of(later)
            for strip in range(STRIPS):
                update(now, values, strip)
                score(later, keys, strip)

        def one(at, _):
            step_on(2 * at)
            step_on(2 * at + 1)
            return 0

        lax.fori_loop(0, todo[0] - 1, one, 0)
        step_on(count - 2)
        last = tile_at(count - 1)
        values = values_of(last)
        for strip in range(STRIPS):
            update(last, values, strip)

    def on_the_diagonal(slot, row):
        def causal(part, strip):
            key_at = lax.broadcasted_iota(jnp.int32, (BLOCK, STRIP), 0)
            token = lax.broadcasted_iota(jnp.int32, (BLOCK, STRIP), 1) + strip * STRIP % BLOCK
            near = jnp.where(key_at <= token, part[:BLOCK], LOWEST)
            return jnp.concatenate([near, jnp.where(z >= 1, part[BLOCK:], LOWEST)], axis=0)

        def far(part, strip):
            return jnp.concatenate(
                [part[:BLOCK], jnp.where(z >= 3, part[BLOCK:], LOWEST)], axis=0
            )

        def alone(pair, mask):
            tile = (slot, row, pair)
            keys, values = keys_of(tile), values_of(tile)
            for strip in range(STRIPS):
                score(tile, keys, strip, mask)
            for strip in range(STRIPS):
                update(tile, values, strip)

        alone(0, causal)
        pl.when(z >= 2)(lambda: alone(1, far))

    if step == 0:
        on_the_diagonal(0, 0)
    if step % 2 == 1:
        pl.when(kv_rows[1] == q_rows[1])(lambda: on_the_diagonal(1, 1))

    index = lax.broadcasted_iota(jnp.int32, (EXT - HEAD_DIM, STRIP), 0)
    for slot in range(2):
        for strip in range(STRIPS):
            at = slice(strip * STRIP, (strip + 1) * STRIP)
            total = acc[slot, strip, HEAD_DIM : HEAD_DIM + 1]
            empty = total == 0.0
            inverse = 1.0 / jnp.where(empty, 1.0, total)
            out_ref[slot, :HEAD_DIM, at] = (acc[slot, strip, :HEAD_DIM] * inverse).astype(
                jnp.bfloat16
            )
            level = best[slot, strip] * SCALE + jnp.log2(jnp.where(empty, 1.0, total))
            high = level.astype(jnp.bfloat16).astype(jnp.float32)
            middle = (level - high).astype(jnp.bfloat16).astype(jnp.float32)
            low = level - high - middle
            rows = jnp.where(index == 0, high, jnp.where(index == 1, middle, low))
            out_ref[slot, HEAD_DIM:, at] = rows.astype(jnp.bfloat16)


def attend(step, place, queries, blocks):
    return pl.pallas_call(
        functools.partial(attend_kernel, step),
        out_shape=jax.ShapeDtypeStruct((2, EXT, ROWS), jnp.bfloat16),
        in_specs=[smem()] + vmem(2),
        out_specs=vmem(1)[0],
        scratch_shapes=[
            pltpu.VMEM((2, STRIPS, 1, STRIP), jnp.float32),
            pltpu.VMEM((2, STRIPS, EXT, STRIP), jnp.float32),
            pltpu.VMEM((STRIPS, 2 * BLOCK, STRIP), jnp.float32),
            pltpu.VMEM((STRIPS, 1, STRIP), jnp.float32),
            pltpu.SMEM((8,), jnp.int32),
        ],
        compiler_params=PARAMS,
        name=f"attend{step}",
    )(place, queries, blocks)


def merge_kernel(place, *refs):
    parts, out_ref = refs[:4], refs[4]
    half = place[0]
    for slot in range(2):
        levels = []
        for part in parts:
            tail = part[slot, HEAD_DIM:].astype(jnp.float32)
            levels.append(tail[0:1] + tail[1:2] + tail[2:3])
        top = jnp.maximum(jnp.maximum(levels[0], levels[1]), jnp.maximum(levels[2], levels[3]))
        shares = [jnp.exp2(level - top) for level in levels]
        inverse = 1.0 / (shares[0] + shares[1] + shares[2] + shares[3])
        mixed = sum(
            part[slot, :HEAD_DIM].astype(jnp.float32) * (share * inverse)
            for part, share in zip(parts, shares)
        )
        row_half = half if slot == 0 else 1 - half
        for sub in range(2):
            for piece in range(4):
                at = sub * BLOCK + piece * 128
                out_ref[piece, row_half, :, sub * 128 : (sub + 1) * 128] = (
                    mixed[:, at : at + 128].T.astype(jnp.bfloat16)
                )


def pinned(value):
    return pltpu.with_memory_space_constraint(value, pltpu.HBM)


def ring(value, axis, steps):
    size = lax.axis_size(axis)
    return lax.ppermute(value, axis, [(at, (at + steps) % size) for at in range(size)])


def routed(value, target):
    pairs = []
    for half in range(2):
        for y in range(4):
            to_half, to_y = target(half, y)
            pairs.append((4 * half + y, 4 * to_half + to_y))
    return lax.ppermute(value, ("xl", "y"), pairs)


def on_device(query_rows, key_rows, value_rows):
    half, y, z = lax.axis_index("xl"), lax.axis_index("y"), lax.axis_index("z")
    place = jnp.stack([half, y, z]).astype(jnp.int32)
    message = jax.ShapeDtypeStruct((ROWS, 128), jnp.bfloat16)
    kv_own, kv_other = pl.pallas_call(
        pack_keys_kernel,
        out_shape=(message,) * 2,
        in_specs=[smem()] + [pl.BlockSpec(memory_space=pltpu.HBM), pl.BlockSpec(memory_space=pltpu.HBM)],
        out_specs=tuple(vmem(2)),
        scratch_shapes=[
            pltpu.VMEM((BLOCK, 256), jnp.bfloat16),
            pltpu.VMEM((BLOCK, 256), jnp.bfloat16),
            pltpu.SemaphoreType.DMA((2,)),
        ],
        compiler_params=PARAMS,
        name="pack_keys",
    )(place, pinned(key_rows), pinned(value_rows))
    q_own, q_other = pl.pallas_call(
        pack_queries_kernel,
        out_shape=(message,) * 2,
        in_specs=[smem()] + [pl.BlockSpec(memory_space=pltpu.HBM), pl.BlockSpec(memory_space=pl.ANY)],
        out_specs=tuple(vmem(2)),
        scratch_shapes=[pltpu.VMEM((BLOCK, 512), jnp.bfloat16), pltpu.SemaphoreType.DMA],
        compiler_params=PARAMS,
        name="pack_queries",
    )(place, pinned(query_rows), kv_own)
    kv_mirror = routed(kv_other, lambda h, r: (1 - h, 3 - r))
    q_swap = ring(q_other, "xl", 1)
    kv_own, _ = lax.optimization_barrier((kv_own, q_other))
    own_near = [ring(kv_own, "z", k) for k in (1, 3)]
    mirror_near = [ring(kv_mirror, "z", k) for k in (1, 3)]
    kv_pair = jnp.stack([kv_own, kv_mirror])
    kv_pair, *near = lax.optimization_barrier((kv_pair, *own_near, *mirror_near))
    own_near, mirror_near = near[:2], near[2:]
    kv_far = ring(kv_pair, "z", 2)
    blocks = jnp.stack(
        [kv_own, own_near[0], kv_far[0], own_near[1]]
        + [kv_mirror, mirror_near[0], kv_far[1], mirror_near[1]]
    )
    q_pair = jnp.stack([q_own, q_swap])
    queries = {0: q_pair, 2: ring(q_pair, "y", 2)}
    queries |= {k: ring(q_pair, "y", k) for k in (3, 1)}
    parts = [ring(attend(k, place, queries[k], blocks), "y", 4 - k) for k in (1, 3, 2)]
    parts.append(attend(0, place, queries[0], blocks))
    merged = pl.pallas_call(
        merge_kernel,
        out_shape=jax.ShapeDtypeStruct((4, 2, 128, 256), jnp.bfloat16),
        in_specs=[smem()] + vmem(4),
        out_specs=vmem(1)[0],
        compiler_params=PARAMS,
        name="merge",
    )(place, *parts)
    merged = merged.reshape(8, 128, 256)
    spread = lax.all_to_all(merged, ("xh", "core", "xl"), split_axis=0, concat_axis=0, tiled=True)
    return spread.transpose(1, 0, 2).reshape(128, 2048)


def solution(mesh):
    fine = Mesh(mesh.devices.reshape(2, 4, 4, 2, 2), ("xl", "y", "z", "xh", "core"))
    tokens, heads = ("xl", "y", "z"), ("xh", "core")
    return jax.shard_map(
        on_device,
        mesh=fine,
        in_specs=(P(tokens, heads),) * 3,
        out_specs=P(tokens + heads, None),
        check_vma=False,
    )
```

```python
import functools

import jax
import jax.numpy as jnp
from jax import lax
from jax.experimental import pallas as pl
from jax.experimental.pallas import tpu as pltpu
from jax.sharding import Mesh, PartitionSpec as P

HEAD_DIM = 128
SCALAR = 168
SCALE = SCALAR ** (-0.5) * 1.4426950408889634
LOWEST = -1e30
BLOCK = 512
ROWS = 2 * BLOCK
EXT = HEAD_DIM + 16
STRIP = 256
STRIPS = ROWS // STRIP

CONTRACT_LAST = (((1,), (1,)), ((), ()))
PARAMS = pltpu.CompilerParams(vmem_limit_bytes=30 * 2**20)


def vmem(count):
    return [pl.BlockSpec(memory_space=pltpu.VMEM)] * count


def smem():
    return pl.BlockSpec(memory_space=pltpu.SMEM)


def pack_kernel(
    place, query_in, key_in, value_in, kv_other, q_other, kv_own, q_own, query_ref, key_ref, value_ref, done
):
    half = place[0]
    copies = [
        pltpu.make_async_copy(key_in, key_ref, done.at[0]),
        pltpu.make_async_copy(value_in, value_ref, done.at[1]),
        pltpu.make_async_copy(query_in, query_ref, done.at[2]),
    ]
    for copy in copies:
        copy.start()
    copies[0].wait()
    for head, kv_out in ((1 - half, kv_other), (half, kv_own)):
        at = pl.multiple_of(head * 128, 128)
        kv_out[:BLOCK] = key_ref[:, pl.ds(at, 128)]
    copies[1].wait()
    for head, kv_out in ((1 - half, kv_other), (half, kv_own)):
        at = pl.multiple_of(head * 128, 128)
        for part in range(4):
            rows = value_ref[part * 128 : (part + 1) * 128, pl.ds(at, 128)]
            kv_out[BLOCK + part * 128 : BLOCK + (part + 1) * 128] = (
                rows.astype(jnp.float32).T.astype(jnp.bfloat16)
            )
    copies[2].wait()
    for head, q_out in ((1 - half, q_other), (half, q_own)):
        for part in range(2):
            at = pl.multiple_of(head * 256 + part * 128, 128)
            q_out[part * BLOCK : (part + 1) * BLOCK] = query_ref[:, pl.ds(at, 128)]


def attend_kernel(step, place, q_ref, kv_ref, out_ref, best, acc, held, peak, todo):
    half, y, z = place[0], place[1], place[2]
    own_row = 4 * half + y
    kv_rows = (own_row, 7 - own_row)
    back = lax.rem(y - step + 4, 4)
    q_rows = (4 * half + back, 4 * (1 - half) + back)

    def keys_of(tile):
        _, row, pair = tile
        at = 4 * row + 2 * pair
        return jnp.concatenate([kv_ref[at + part, :BLOCK] for part in range(2)], axis=0)

    def values_of(tile):
        _, row, pair = tile
        at = 4 * row + 2 * pair
        flipped = [
            kv_ref[at + part, BLOCK + piece * 128 : BLOCK + (piece + 1) * 128]
            for part in range(2)
            for piece in range(4)
        ]
        ones = jnp.ones((EXT - HEAD_DIM, 2 * BLOCK), jnp.bfloat16)
        return jnp.concatenate([jnp.concatenate(flipped, axis=1), ones], axis=0)

    def score(tile, keys, strip, mask=None):
        part = lax.dot_general(
            keys,
            q_ref[tile[0], strip * STRIP : (strip + 1) * STRIP],
            CONTRACT_LAST,
            preferred_element_type=jnp.float32,
        )
        if mask is not None:
            part = mask(part, strip)
        held[strip] = part
        peak[strip] = jnp.max(part, axis=0, keepdims=True)

    def update(tile, values, strip):
        slot = tile[0]
        old = best[slot, strip]
        new = jnp.maximum(old, peak[strip])
        weights = jnp.exp2(held[strip] * SCALE - new * SCALE)
        rescale = jnp.exp2((old - new) * SCALE)
        best[slot, strip] = new
        acc[slot, strip] = acc[slot, strip] * rescale + jnp.dot(
            values, weights.astype(jnp.bfloat16), preferred_element_type=jnp.float32
        )

    best[...] = jnp.full_like(best, LOWEST)
    acc[...] = jnp.zeros_like(acc)
    todo[0] = 0
    for slot in range(2):
        for row in range(2):

            @pl.when(kv_rows[row] < q_rows[slot])
            def _():
                count = todo[0]
                todo[1 + count] = 2 * slot + row
                todo[0] = count + 1

    def tile_at(at):
        entry = todo[1 + at // 2]
        return entry // 2, entry % 2, at % 2

    count = 2 * todo[0]

    @pl.when(count > 0)
    def _():
        start = tile_at(0)
        keys = keys_of(start)
        for strip in range(STRIPS):
            score(start, keys, strip)

        def step_on(at):
            now, later = tile_at(at), tile_at(at + 1)
            values, keys = values_of(now), keys_of(later)
            for strip in range(STRIPS):
                update(now, values, strip)
                score(later, keys, strip)

        def one(at, _):
            step_on(2 * at)
            step_on(2 * at + 1)
            return 0

        lax.fori_loop(0, todo[0] - 1, one, 0)
        step_on(count - 2)
        last = tile_at(count - 1)
        values = values_of(last)
        for strip in range(STRIPS):
            update(last, values, strip)

    def on_the_diagonal(slot, row):
        def causal(part, strip):
            key_at = lax.broadcasted_iota(jnp.int32, (BLOCK, STRIP), 0)
            token = lax.broadcasted_iota(jnp.int32, (BLOCK, STRIP), 1) + strip * STRIP % BLOCK
            near = jnp.where(key_at <= token, part[:BLOCK], LOWEST)
            return jnp.concatenate([near, jnp.where(z >= 1, part[BLOCK:], LOWEST)], axis=0)

        def far(part, strip):
            return jnp.concatenate(
                [jnp.where(z >= 3, part[:BLOCK], LOWEST), part[BLOCK:]], axis=0
            )

        def alone(pair, mask):
            tile = (slot, row, pair)
            keys, values = keys_of(tile), values_of(tile)
            for strip in range(STRIPS):
                score(tile, keys, strip, mask)
            for strip in range(STRIPS):
                update(tile, values, strip)

        alone(0, causal)
        pl.when(z >= 2)(lambda: alone(1, far))

    if step == 0:
        on_the_diagonal(0, 0)
    if step % 2 == 1:
        pl.when(kv_rows[1] == q_rows[1])(lambda: on_the_diagonal(1, 1))

    index = lax.broadcasted_iota(jnp.int32, (EXT - HEAD_DIM, STRIP), 0)
    for slot in range(2):
        for strip in range(STRIPS):
            at = slice(strip * STRIP, (strip + 1) * STRIP)
            total = acc[slot, strip, HEAD_DIM : HEAD_DIM + 1]
            empty = total == 0.0
            inverse = 1.0 / jnp.where(empty, 1.0, total)
            out_ref[slot, :HEAD_DIM, at] = (acc[slot, strip, :HEAD_DIM] * inverse).astype(
                jnp.bfloat16
            )
            level = best[slot, strip] * SCALE + jnp.log2(jnp.where(empty, 1.0, total))
            high = level.astype(jnp.bfloat16).astype(jnp.float32)
            middle = (level - high).astype(jnp.bfloat16).astype(jnp.float32)
            low = level - high - middle
            rows = jnp.where(index == 0, high, jnp.where(index == 1, middle, low))
            out_ref[slot, HEAD_DIM:, at] = rows.astype(jnp.bfloat16)


def attend(step, place, queries, blocks):
    return pl.pallas_call(
        functools.partial(attend_kernel, step),
        out_shape=jax.ShapeDtypeStruct((2, EXT, ROWS), jnp.bfloat16),
        in_specs=[smem()] + vmem(2),
        out_specs=vmem(1)[0],
        scratch_shapes=[
            pltpu.VMEM((2, STRIPS, 1, STRIP), jnp.float32),
            pltpu.VMEM((2, STRIPS, EXT, STRIP), jnp.float32),
            pltpu.VMEM((STRIPS, 2 * BLOCK, STRIP), jnp.float32),
            pltpu.VMEM((STRIPS, 1, STRIP), jnp.float32),
            pltpu.SMEM((8,), jnp.int32),
        ],
        compiler_params=PARAMS,
        name=f"attend{step}",
    )(place, queries, blocks)


def merge_kernel(place, *refs):
    parts, out_ref = refs[:4], refs[4]
    half = place[0]
    for slot in range(2):
        levels = []
        for part in parts:
            tail = part[slot, HEAD_DIM:].astype(jnp.float32)
            levels.append(tail[0:1] + tail[1:2] + tail[2:3])
        top = jnp.maximum(jnp.maximum(levels[0], levels[1]), jnp.maximum(levels[2], levels[3]))
        shares = [jnp.exp2(level - top) for level in levels]
        inverse = 1.0 / (shares[0] + shares[1] + shares[2] + shares[3])
        mixed = sum(
            part[slot, :HEAD_DIM].astype(jnp.float32) * (share * inverse)
            for part, share in zip(parts, shares)
        )
        row_half = half if slot == 0 else 1 - half
        for sub in range(2):
            for piece in range(4):
                at = sub * BLOCK + piece * 128
                out_ref[piece, row_half, :, sub * 128 : (sub + 1) * 128] = (
                    mixed[:, at : at + 128].T.astype(jnp.bfloat16)
                )


def pinned(value):
    return pltpu.with_memory_space_constraint(value, pltpu.HBM)


def ring(value, axis, steps):
    size = lax.axis_size(axis)
    return lax.ppermute(value, axis, [(at, (at + steps) % size) for at in range(size)])


def routed(value, target):
    pairs = []
    for half in range(2):
        for y in range(4):
            to_half, to_y = target(half, y)
            pairs.append((4 * half + y, 4 * to_half + to_y))
    return lax.ppermute(value, ("xl", "y"), pairs)


def on_device(query_rows, key_rows, value_rows):
    half, y, z = lax.axis_index("xl"), lax.axis_index("y"), lax.axis_index("z")
    place = jnp.stack([half, y, z]).astype(jnp.int32)
    message = jax.ShapeDtypeStruct((ROWS, 128), jnp.bfloat16)
    kv_other, q_other, kv_own, q_own = pl.pallas_call(
        pack_kernel,
        out_shape=(message,) * 4,
        in_specs=[smem()] + [pl.BlockSpec(memory_space=pltpu.HBM)] * 3,
        out_specs=tuple(vmem(4)),
        scratch_shapes=[
            pltpu.VMEM((BLOCK, 512), jnp.bfloat16),
            pltpu.VMEM((BLOCK, 256), jnp.bfloat16),
            pltpu.VMEM((BLOCK, 256), jnp.bfloat16),
            pltpu.SemaphoreType.DMA((3,)),
        ],
        compiler_params=PARAMS,
        name="pack",
    )(place, pinned(query_rows), pinned(key_rows), pinned(value_rows))
    kv_mirror = routed(kv_other, lambda h, r: (1 - h, 3 - r))
    q_swap = ring(q_other, "xl", 1)
    kv_pair = jnp.stack([kv_own, kv_mirror])
    pairs = {0: kv_pair}
    pairs |= {k: ring(kv_pair, "z", k) for k in (2, 3, 1)}
    blocks = jnp.concatenate(
        [pairs[k][row : row + 1] for row in range(2) for k in (0, 1, 3, 2)], axis=0
    )
    q_pair = jnp.stack([q_own, q_swap])
    queries = {0: q_pair}
    queries |= {k: ring(q_pair, "y", k) for k in (1, 3, 2)}
    parts = [ring(attend(k, place, queries[k], blocks), "y", 4 - k) for k in (1, 3, 2)]
    parts.append(attend(0, place, queries[0], blocks))
    merged = pl.pallas_call(
        merge_kernel,
        out_shape=jax.ShapeDtypeStruct((4, 2, 128, 256), jnp.bfloat16),
        in_specs=[smem()] + vmem(4),
        out_specs=vmem(1)[0],
        compiler_params=PARAMS,
        name="merge",
    )(place, *parts)
    merged = merged.reshape(8, 128, 256)
    spread = lax.all_to_all(merged, ("xh", "core", "xl"), split_axis=0, concat_axis=0, tiled=True)
    return spread.transpose(1, 0, 2).reshape(128, 2048)


def solution(mesh):
    fine = Mesh(mesh.devices.reshape(2, 4, 4, 2, 2), ("xl", "y", "z", "xh", "core"))
    tokens, heads = ("xl", "y", "z"), ("xh", "core")
    return jax.shard_map(
        on_device,
        mesh=fine,
        in_specs=(P(tokens, heads),) * 3,
        out_specs=P(tokens + heads, None),
        check_vma=False,
    )
```

```python
import functools

import jax
import jax.numpy as jnp
from jax import lax
from jax.experimental import pallas as pl
from jax.experimental.pallas import tpu as pltpu
from jax.sharding import Mesh, PartitionSpec as P

HEAD_DIM = 128
SCALAR = 168
SCALE = SCALAR ** (-0.5) * 1.4426950408889634
LOWEST = -1e30
BLOCK = 512
ROWS = 2 * BLOCK
EXT = HEAD_DIM + 16
STRIP = 256
STRIPS = ROWS // STRIP

CONTRACT_LAST = (((1,), (1,)), ((), ()))
PARAMS = pltpu.CompilerParams(vmem_limit_bytes=30 * 2**20)


def vmem(count):
    return [pl.BlockSpec(memory_space=pltpu.VMEM)] * count


def smem():
    return pl.BlockSpec(memory_space=pltpu.SMEM)


def pack_kernel(
    place, query_in, key_in, value_in, kv_other, q_other, kv_own, q_own, query_ref, key_ref, value_ref, done
):
    half = place[0]
    copies = [
        pltpu.make_async_copy(key_in, key_ref, done.at[0]),
        pltpu.make_async_copy(value_in, value_ref, done.at[1]),
        pltpu.make_async_copy(query_in, query_ref, done.at[2]),
    ]
    for copy in copies:
        copy.start()
    copies[0].wait()
    for head, kv_out in ((1 - half, kv_other), (half, kv_own)):
        at = pl.multiple_of(head * 128, 128)
        kv_out[:BLOCK] = key_ref[:, pl.ds(at, 128)]
    copies[1].wait()
    for head, kv_out in ((1 - half, kv_other), (half, kv_own)):
        at = pl.multiple_of(head * 128, 128)
        for part in range(4):
            rows = value_ref[part * 128 : (part + 1) * 128, pl.ds(at, 128)]
            kv_out[BLOCK + part * 128 : BLOCK + (part + 1) * 128] = (
                rows.astype(jnp.float32).T.astype(jnp.bfloat16)
            )
    copies[2].wait()
    for head, q_out in ((1 - half, q_other), (half, q_own)):
        for part in range(2):
            at = pl.multiple_of(head * 256 + part * 128, 128)
            q_out[part * BLOCK : (part + 1) * BLOCK] = query_ref[:, pl.ds(at, 128)]


def attend_kernel(step, place, q_ref, kv_ref, out_ref, best, acc, held, peak, todo):
    half, y, z = place[0], place[1], place[2]
    own_row = 4 * half + y
    kv_rows = (own_row, 7 - own_row)
    back = lax.rem(y - step + 4, 4)
    q_rows = (4 * half + back, 4 * (1 - half) + back)

    def keys_of(tile):
        _, row, pair = tile
        at = 4 * row + 2 * pair
        return jnp.concatenate([kv_ref[at + part, :BLOCK] for part in range(2)], axis=0)

    def values_of(tile):
        _, row, pair = tile
        at = 4 * row + 2 * pair
        flipped = [
            kv_ref[at + part, BLOCK + piece * 128 : BLOCK + (piece + 1) * 128]
            for part in range(2)
            for piece in range(4)
        ]
        ones = jnp.ones((EXT - HEAD_DIM, 2 * BLOCK), jnp.bfloat16)
        return jnp.concatenate([jnp.concatenate(flipped, axis=1), ones], axis=0)

    def score(tile, keys, strip, mask=None):
        part = lax.dot_general(
            keys,
            q_ref[tile[0], strip * STRIP : (strip + 1) * STRIP],
            CONTRACT_LAST,
            preferred_element_type=jnp.float32,
        )
        if mask is not None:
            part = mask(part, strip)
        held[strip] = part
        peak[strip] = jnp.max(part, axis=0, keepdims=True)

    def update(tile, values, strip):
        slot = tile[0]
        old = best[slot, strip]
        new = jnp.maximum(old, peak[strip])
        weights = jnp.exp2(held[strip] * SCALE - new * SCALE)
        rescale = jnp.exp2((old - new) * SCALE)
        best[slot, strip] = new
        acc[slot, strip] = acc[slot, strip] * rescale + jnp.dot(
            values, weights.astype(jnp.bfloat16), preferred_element_type=jnp.float32
        )

    best[...] = jnp.full_like(best, LOWEST)
    acc[...] = jnp.zeros_like(acc)
    todo[0] = 0
    for slot in range(2):
        for row in range(2):

            @pl.when(kv_rows[row] < q_rows[slot])
            def _():
                count = todo[0]
                todo[1 + count] = 2 * slot + row
                todo[0] = count + 1

    def tile_at(at):
        entry = todo[1 + at // 2]
        return entry // 2, entry % 2, at % 2

    count = 2 * todo[0]

    @pl.when(count > 0)
    def _():
        start = tile_at(0)
        keys = keys_of(start)
        for strip in range(STRIPS):
            score(start, keys, strip)

        def step_on(at):
            now, later = tile_at(at), tile_at(at + 1)
            values, keys = values_of(now), keys_of(later)
            for strip in range(STRIPS):
                update(now, values, strip)
                score(later, keys, strip)

        def one(at, _):
            step_on(2 * at)
            step_on(2 * at + 1)
            return 0

        lax.fori_loop(0, todo[0] - 1, one, 0)
        step_on(count - 2)
        last = tile_at(count - 1)
        values = values_of(last)
        for strip in range(STRIPS):
            update(last, values, strip)

    def on_the_diagonal(slot, row):
        def causal(part, strip):
            key_at = lax.broadcasted_iota(jnp.int32, (BLOCK, STRIP), 0)
            token = lax.broadcasted_iota(jnp.int32, (BLOCK, STRIP), 1) + strip * STRIP % BLOCK
            near = jnp.where(key_at <= token, part[:BLOCK], LOWEST)
            return jnp.concatenate([near, jnp.where(z >= 1, part[BLOCK:], LOWEST)], axis=0)

        def far(part, strip):
            return jnp.concatenate(
                [jnp.where(z >= 3, part[:BLOCK], LOWEST), part[BLOCK:]], axis=0
            )

        def alone(pair, mask):
            tile = (slot, row, pair)
            keys, values = keys_of(tile), values_of(tile)
            for strip in range(STRIPS):
                score(tile, keys, strip, mask)
            for strip in range(STRIPS):
                update(tile, values, strip)

        alone(0, causal)
        pl.when(z >= 2)(lambda: alone(1, far))

    if step == 0:
        on_the_diagonal(0, 0)
    if step % 2 == 1:
        pl.when(kv_rows[1] == q_rows[1])(lambda: on_the_diagonal(1, 1))

    index = lax.broadcasted_iota(jnp.int32, (EXT - HEAD_DIM, STRIP), 0)
    for slot in range(2):
        for strip in range(STRIPS):
            at = slice(strip * STRIP, (strip + 1) * STRIP)
            total = acc[slot, strip, HEAD_DIM : HEAD_DIM + 1]
            empty = total == 0.0
            inverse = 1.0 / jnp.where(empty, 1.0, total)
            out_ref[slot, :HEAD_DIM, at] = (acc[slot, strip, :HEAD_DIM] * inverse).astype(
                jnp.bfloat16
            )
            level = best[slot, strip] * SCALE + jnp.log2(jnp.where(empty, 1.0, total))
            high = level.astype(jnp.bfloat16).astype(jnp.float32)
            middle = (level - high).astype(jnp.bfloat16).astype(jnp.float32)
            low = level - high - middle
            rows = jnp.where(index == 0, high, jnp.where(index == 1, middle, low))
            out_ref[slot, HEAD_DIM:, at] = rows.astype(jnp.bfloat16)


def attend(step, place, queries, blocks):
    return pl.pallas_call(
        functools.partial(attend_kernel, step),
        out_shape=jax.ShapeDtypeStruct((2, EXT, ROWS), jnp.bfloat16),
        in_specs=[smem()] + vmem(2),
        out_specs=vmem(1)[0],
        scratch_shapes=[
            pltpu.VMEM((2, STRIPS, 1, STRIP), jnp.float32),
            pltpu.VMEM((2, STRIPS, EXT, STRIP), jnp.float32),
            pltpu.VMEM((STRIPS, 2 * BLOCK, STRIP), jnp.float32),
            pltpu.VMEM((STRIPS, 1, STRIP), jnp.float32),
            pltpu.SMEM((8,), jnp.int32),
        ],
        compiler_params=PARAMS,
        name=f"attend{step}",
    )(place, queries, blocks)


def merge_kernel(place, *refs):
    parts, out_ref = refs[:4], refs[4]
    half = place[0]
    for slot in range(2):
        levels = []
        for part in parts:
            tail = part[slot, HEAD_DIM:].astype(jnp.float32)
            levels.append(tail[0:1] + tail[1:2] + tail[2:3])
        top = jnp.maximum(jnp.maximum(levels[0], levels[1]), jnp.maximum(levels[2], levels[3]))
        shares = [jnp.exp2(level - top) for level in levels]
        inverse = 1.0 / (shares[0] + shares[1] + shares[2] + shares[3])
        mixed = sum(
            part[slot, :HEAD_DIM].astype(jnp.float32) * (share * inverse)
            for part, share in zip(parts, shares)
        )
        row_half = half if slot == 0 else 1 - half
        for sub in range(2):
            for piece in range(4):
                at = sub * BLOCK + piece * 128
                out_ref[piece, row_half, :, sub * 128 : (sub + 1) * 128] = (
                    mixed[:, at : at + 128].T.astype(jnp.bfloat16)
                )


def pinned(value):
    return pltpu.with_memory_space_constraint(value, pltpu.HBM)


def ring(value, axis, steps):
    size = lax.axis_size(axis)
    return lax.ppermute(value, axis, [(at, (at + steps) % size) for at in range(size)])


def routed(value, target):
    pairs = []
    for half in range(2):
        for y in range(4):
            to_half, to_y = target(half, y)
            pairs.append((4 * half + y, 4 * to_half + to_y))
    return lax.ppermute(value, ("xl", "y"), pairs)


def on_device(query_rows, key_rows, value_rows):
    half, y, z = lax.axis_index("xl"), lax.axis_index("y"), lax.axis_index("z")
    place = jnp.stack([half, y, z]).astype(jnp.int32)
    message = jax.ShapeDtypeStruct((ROWS, 128), jnp.bfloat16)
    kv_other, q_other, kv_own, q_own = pl.pallas_call(
        pack_kernel,
        out_shape=(message,) * 4,
        in_specs=[smem()] + [pl.BlockSpec(memory_space=pltpu.HBM)] * 3,
        out_specs=tuple(vmem(4)),
        scratch_shapes=[
            pltpu.VMEM((BLOCK, 512), jnp.bfloat16),
            pltpu.VMEM((BLOCK, 256), jnp.bfloat16),
            pltpu.VMEM((BLOCK, 256), jnp.bfloat16),
            pltpu.SemaphoreType.DMA((3,)),
        ],
        compiler_params=PARAMS,
        name="pack",
    )(place, pinned(query_rows), pinned(key_rows), pinned(value_rows))
    kv_mirror = routed(kv_other, lambda h, r: (1 - h, 3 - r))
    q_swap = ring(q_other, "xl", 1)
    kv_pair = jnp.stack([kv_own, kv_mirror])
    pairs = {0: kv_pair}
    pairs |= {k: ring(kv_pair, "z", k) for k in (2, 3, 1)}
    blocks = jnp.concatenate(
        [pairs[k][row : row + 1] for row in range(2) for k in (0, 1, 3, 2)], axis=0
    )
    q_pair = jnp.stack([q_own, q_swap])
    queries = {0: q_pair}
    queries |= {k: ring(q_pair, "y", k) for k in (3, 1, 2)}
    parts = [ring(attend(k, place, queries[k], blocks), "y", 4 - k) for k in (3, 1, 2)]
    parts.append(attend(0, place, queries[0], blocks))
    merged = pl.pallas_call(
        merge_kernel,
        out_shape=jax.ShapeDtypeStruct((4, 2, 128, 256), jnp.bfloat16),
        in_specs=[smem()] + vmem(4),
        out_specs=vmem(1)[0],
        compiler_params=PARAMS,
        name="merge",
    )(place, *parts)
    merged = merged.reshape(8, 128, 256)
    spread = lax.all_to_all(merged, ("xh", "core", "xl"), split_axis=0, concat_axis=0, tiled=True)
    return spread.transpose(1, 0, 2).reshape(128, 2048)


def solution(mesh):
    fine = Mesh(mesh.devices.reshape(2, 4, 4, 2, 2), ("xl", "y", "z", "xh", "core"))
    tokens, heads = ("xl", "y", "z"), ("xh", "core")
    return jax.shard_map(
        on_device,
        mesh=fine,
        in_specs=(P(tokens, heads),) * 3,
        out_specs=P(tokens + heads, None),
        check_vma=False,
    )
```

```python
import functools

import jax
import jax.numpy as jnp
from jax import lax
from jax.experimental import pallas as pl
from jax.experimental.pallas import tpu as pltpu
from jax.sharding import Mesh, PartitionSpec as P

HEAD_DIM = 128
SCALAR = 168
SCALE = SCALAR ** (-0.5) * 1.4426950408889634
LOWEST = -1e30
BLOCK = 512
ROWS = 2 * BLOCK
EXT = HEAD_DIM + 16
STRIP = 256
STRIPS = ROWS // STRIP

CONTRACT_LAST = (((1,), (1,)), ((), ()))
PARAMS = pltpu.CompilerParams(vmem_limit_bytes=30 * 2**20)


def vmem(count):
    return [pl.BlockSpec(memory_space=pltpu.VMEM)] * count


def smem():
    return pl.BlockSpec(memory_space=pltpu.SMEM)


def pack_kernel(
    place, query_in, key_in, value_in, kv_other, q_other, kv_own, q_own, query_ref, key_ref, value_ref, done
):
    half = place[0]
    copies = [
        pltpu.make_async_copy(key_in, key_ref, done.at[0]),
        pltpu.make_async_copy(value_in, value_ref, done.at[1]),
        pltpu.make_async_copy(query_in, query_ref, done.at[2]),
    ]
    for copy in copies:
        copy.start()
    copies[0].wait()
    for head, kv_out in ((1 - half, kv_other), (half, kv_own)):
        at = pl.multiple_of(head * 128, 128)
        kv_out[:BLOCK] = key_ref[:, pl.ds(at, 128)]
    copies[1].wait()
    for head, kv_out in ((1 - half, kv_other), (half, kv_own)):
        at = pl.multiple_of(head * 128, 128)
        for part in range(4):
            rows = value_ref[part * 128 : (part + 1) * 128, pl.ds(at, 128)]
            kv_out[BLOCK + part * 128 : BLOCK + (part + 1) * 128] = (
                rows.astype(jnp.float32).T.astype(jnp.bfloat16)
            )
    copies[2].wait()
    for head, q_out in ((1 - half, q_other), (half, q_own)):
        for part in range(2):
            at = pl.multiple_of(head * 256 + part * 128, 128)
            q_out[part * BLOCK : (part + 1) * BLOCK] = query_ref[:, pl.ds(at, 128)]


def attend_kernel(step, place, q_ref, kv_ref, out_ref, best, acc, held, peak, todo):
    half, y, z = place[0], place[1], place[2]
    own_row = 4 * half + y
    kv_rows = (own_row, 7 - own_row)
    back = lax.rem(y - step + 4, 4)
    q_rows = (4 * half + back, 4 * (1 - half) + back)

    def keys_of(tile):
        _, row, pair = tile
        at = 4 * row + 2 * pair
        return jnp.concatenate([kv_ref[at + part, :BLOCK] for part in range(2)], axis=0)

    def values_of(tile):
        _, row, pair = tile
        at = 4 * row + 2 * pair
        flipped = [
            kv_ref[at + part, BLOCK + piece * 128 : BLOCK + (piece + 1) * 128]
            for part in range(2)
            for piece in range(4)
        ]
        ones = jnp.ones((EXT - HEAD_DIM, 2 * BLOCK), jnp.bfloat16)
        return jnp.concatenate([jnp.concatenate(flipped, axis=1), ones], axis=0)

    def score(tile, keys, strip, mask=None):
        part = lax.dot_general(
            keys,
            q_ref[tile[0], strip * STRIP : (strip + 1) * STRIP],
            CONTRACT_LAST,
            preferred_element_type=jnp.float32,
        )
        if mask is not None:
            part = mask(part, strip)
        held[strip] = part
        peak[strip] = jnp.max(part, axis=0, keepdims=True)

    def update(tile, values, strip):
        slot = tile[0]
        old = best[slot, strip]
        new = jnp.maximum(old, peak[strip])
        weights = jnp.exp2(held[strip] * SCALE - new * SCALE)
        rescale = jnp.exp2((old - new) * SCALE)
        best[slot, strip] = new
        acc[slot, strip] = acc[slot, strip] * rescale + jnp.dot(
            values, weights.astype(jnp.bfloat16), preferred_element_type=jnp.float32
        )

    best[...] = jnp.full_like(best, LOWEST)
    acc[...] = jnp.zeros_like(acc)
    todo[0] = 0
    for slot in range(2):
        for row in range(2):

            @pl.when(kv_rows[row] < q_rows[slot])
            def _():
                count = todo[0]
                todo[1 + count] = 2 * slot + row
                todo[0] = count + 1

    def tile_at(at):
        entry = todo[1 + at // 2]
        return entry // 2, entry % 2, at % 2

    count = 2 * todo[0]

    @pl.when(count > 0)
    def _():
        start = tile_at(0)
        keys = keys_of(start)
        for strip in range(STRIPS):
            score(start, keys, strip)

        def step_on(at):
            now, later = tile_at(at), tile_at(at + 1)
            values, keys = values_of(now), keys_of(later)
            for strip in range(STRIPS):
                update(now, values, strip)
                score(later, keys, strip)

        def one(at, _):
            step_on(2 * at)
            step_on(2 * at + 1)
            return 0

        lax.fori_loop(0, todo[0] - 1, one, 0)
        step_on(count - 2)
        last = tile_at(count - 1)
        values = values_of(last)
        for strip in range(STRIPS):
            update(last, values, strip)

    def on_the_diagonal(slot, row):
        def causal(part, strip):
            key_at = lax.broadcasted_iota(jnp.int32, (BLOCK, STRIP), 0)
            token = lax.broadcasted_iota(jnp.int32, (BLOCK, STRIP), 1) + strip * STRIP % BLOCK
            near = jnp.where(key_at <= token, part[:BLOCK], LOWEST)
            return jnp.concatenate([near, jnp.where(z >= 1, part[BLOCK:], LOWEST)], axis=0)

        def far(part, strip):
            return jnp.concatenate(
                [jnp.where(z >= 3, part[:BLOCK], LOWEST), part[BLOCK:]], axis=0
            )

        def alone(pair, mask):
            tile = (slot, row, pair)
            keys, values = keys_of(tile), values_of(tile)
            for strip in range(STRIPS):
                score(tile, keys, strip, mask)
            for strip in range(STRIPS):
                update(tile, values, strip)

        alone(0, causal)
        pl.when(z >= 2)(lambda: alone(1, far))

    if step == 0:
        on_the_diagonal(0, 0)
    if step % 2 == 1:
        pl.when(kv_rows[1] == q_rows[1])(lambda: on_the_diagonal(1, 1))

    index = lax.broadcasted_iota(jnp.int32, (EXT - HEAD_DIM, STRIP), 0)
    for slot in range(2):
        for strip in range(STRIPS):
            at = slice(strip * STRIP, (strip + 1) * STRIP)
            total = acc[slot, strip, HEAD_DIM : HEAD_DIM + 1]
            empty = total == 0.0
            inverse = 1.0 / jnp.where(empty, 1.0, total)
            out_ref[slot, :HEAD_DIM, at] = (acc[slot, strip, :HEAD_DIM] * inverse).astype(
                jnp.bfloat16
            )
            level = best[slot, strip] * SCALE + jnp.log2(jnp.where(empty, 1.0, total))
            high = level.astype(jnp.bfloat16).astype(jnp.float32)
            middle = (level - high).astype(jnp.bfloat16).astype(jnp.float32)
            low = level - high - middle
            rows = jnp.where(index == 0, high, jnp.where(index == 1, middle, low))
            out_ref[slot, HEAD_DIM:, at] = rows.astype(jnp.bfloat16)


def attend(step, place, queries, blocks):
    return pl.pallas_call(
        functools.partial(attend_kernel, step),
        out_shape=jax.ShapeDtypeStruct((2, EXT, ROWS), jnp.bfloat16),
        in_specs=[smem()] + vmem(2),
        out_specs=vmem(1)[0],
        scratch_shapes=[
            pltpu.VMEM((2, STRIPS, 1, STRIP), jnp.float32),
            pltpu.VMEM((2, STRIPS, EXT, STRIP), jnp.float32),
            pltpu.VMEM((STRIPS, 2 * BLOCK, STRIP), jnp.float32),
            pltpu.VMEM((STRIPS, 1, STRIP), jnp.float32),
            pltpu.SMEM((8,), jnp.int32),
        ],
        compiler_params=PARAMS,
        name=f"attend{step}",
    )(place, queries, blocks)


def merge_kernel(place, *refs):
    parts, out_ref = refs[:4], refs[4]
    half = place[0]
    for slot in range(2):
        levels = []
        for part in parts:
            tail = part[slot, HEAD_DIM:].astype(jnp.float32)
            levels.append(tail[0:1] + tail[1:2] + tail[2:3])
        top = jnp.maximum(jnp.maximum(levels[0], levels[1]), jnp.maximum(levels[2], levels[3]))
        shares = [jnp.exp2(level - top) for level in levels]
        inverse = 1.0 / (shares[0] + shares[1] + shares[2] + shares[3])
        mixed = sum(
            part[slot, :HEAD_DIM].astype(jnp.float32) * (share * inverse)
            for part, share in zip(parts, shares)
        )
        row_half = half if slot == 0 else 1 - half
        for sub in range(2):
            for piece in range(4):
                at = sub * BLOCK + piece * 128
                out_ref[piece, row_half, :, sub * 128 : (sub + 1) * 128] = (
                    mixed[:, at : at + 128].T.astype(jnp.bfloat16)
                )


def pinned(value):
    return pltpu.with_memory_space_constraint(value, pltpu.HBM)


def ring(value, axis, steps):
    size = lax.axis_size(axis)
    return lax.ppermute(value, axis, [(at, (at + steps) % size) for at in range(size)])


def routed(value, target):
    pairs = []
    for half in range(2):
        for y in range(4):
            to_half, to_y = target(half, y)
            pairs.append((4 * half + y, 4 * to_half + to_y))
    return lax.ppermute(value, ("xl", "y"), pairs)


def on_device(query_rows, key_rows, value_rows):
    half, y, z = lax.axis_index("xl"), lax.axis_index("y"), lax.axis_index("z")
    place = jnp.stack([half, y, z]).astype(jnp.int32)
    message = jax.ShapeDtypeStruct((ROWS, 128), jnp.bfloat16)
    kv_other, q_other, kv_own, q_own = pl.pallas_call(
        pack_kernel,
        out_shape=(message,) * 4,
        in_specs=[smem()] + [pl.BlockSpec(memory_space=pltpu.HBM)] * 3,
        out_specs=tuple(vmem(4)),
        scratch_shapes=[
            pltpu.VMEM((BLOCK, 512), jnp.bfloat16),
            pltpu.VMEM((BLOCK, 256), jnp.bfloat16),
            pltpu.VMEM((BLOCK, 256), jnp.bfloat16),
            pltpu.SemaphoreType.DMA((3,)),
        ],
        compiler_params=PARAMS,
        name="pack",
    )(place, pinned(query_rows), pinned(key_rows), pinned(value_rows))
    kv_mirror = routed(kv_other, lambda h, r: (1 - h, 3 - r))
    q_swap = ring(q_other, "xl", 1)
    q_early = ring(q_own, "y", 3)
    kv_mirror, q_early = lax.optimization_barrier((kv_mirror, q_early))
    kv_pair = jnp.stack([kv_own, kv_mirror])
    pairs = {0: kv_pair}
    pairs |= {k: ring(kv_pair, "z", k) for k in (2, 3, 1)}
    blocks = jnp.concatenate(
        [pairs[k][row : row + 1] for row in range(2) for k in (0, 1, 3, 2)], axis=0
    )
    q_pair = jnp.stack([q_own, q_swap])
    queries = {0: q_pair}
    queries[1] = ring(q_pair, "y", 1)
    queries[3] = jnp.stack([q_early, ring(q_swap, "y", 3)])
    queries[2] = ring(q_pair, "y", 2)
    parts = [ring(attend(k, place, queries[k], blocks), "y", 4 - k) for k in (1, 3, 2)]
    parts.append(attend(0, place, queries[0], blocks))
    merged = pl.pallas_call(
        merge_kernel,
        out_shape=jax.ShapeDtypeStruct((4, 2, 128, 256), jnp.bfloat16),
        in_specs=[smem()] + vmem(4),
        out_specs=vmem(1)[0],
        compiler_params=PARAMS,
        name="merge",
    )(place, *parts)
    merged = merged.reshape(8, 128, 256)
    spread = lax.all_to_all(merged, ("xh", "core", "xl"), split_axis=0, concat_axis=0, tiled=True)
    return spread.transpose(1, 0, 2).reshape(128, 2048)


def solution(mesh):
    fine = Mesh(mesh.devices.reshape(2, 4, 4, 2, 2), ("xl", "y", "z", "xh", "core"))
    tokens, heads = ("xl", "y", "z"), ("xh", "core")
    return jax.shard_map(
        on_device,
        mesh=fine,
        in_specs=(P(tokens, heads),) * 3,
        out_specs=P(tokens + heads, None),
        check_vma=False,
    )
```

```python
import functools

import jax
import jax.numpy as jnp
from jax import lax
from jax.experimental import pallas as pl
from jax.experimental.pallas import tpu as pltpu
from jax.sharding import Mesh, PartitionSpec as P

HEAD_DIM = 128
SCALAR = 168
SCALE = SCALAR ** (-0.5) * 1.4426950408889634
LOWEST = -1e30
BLOCK = 512
ROWS = 2 * BLOCK
EXT = HEAD_DIM + 16
STRIP = 256
STRIPS = ROWS // STRIP

CONTRACT_LAST = (((1,), (1,)), ((), ()))
PARAMS = pltpu.CompilerParams(vmem_limit_bytes=30 * 2**20)


def vmem(count):
    return [pl.BlockSpec(memory_space=pltpu.VMEM)] * count


def smem():
    return pl.BlockSpec(memory_space=pltpu.SMEM)


def pack_kernel(
    place, query_in, key_in, value_in, kv_other, q_other, kv_own, q_own, query_ref, key_ref, value_ref, done
):
    half = place[0]
    copies = [
        pltpu.make_async_copy(key_in, key_ref, done.at[0]),
        pltpu.make_async_copy(value_in, value_ref, done.at[1]),
        pltpu.make_async_copy(query_in, query_ref, done.at[2]),
    ]
    for copy in copies:
        copy.start()
    copies[0].wait()
    for head, kv_out in ((1 - half, kv_other), (half, kv_own)):
        at = pl.multiple_of(head * 128, 128)
        kv_out[:BLOCK] = key_ref[:, pl.ds(at, 128)]
    copies[1].wait()
    for head, kv_out in ((1 - half, kv_other), (half, kv_own)):
        at = pl.multiple_of(head * 128, 128)
        for part in range(4):
            rows = value_ref[part * 128 : (part + 1) * 128, pl.ds(at, 128)]
            kv_out[BLOCK + part * 128 : BLOCK + (part + 1) * 128] = (
                rows.astype(jnp.float32).T.astype(jnp.bfloat16)
            )
    copies[2].wait()
    for head, q_out in ((1 - half, q_other), (half, q_own)):
        for part in range(2):
            at = pl.multiple_of(head * 256 + part * 128, 128)
            q_out[part * BLOCK : (part + 1) * BLOCK] = query_ref[:, pl.ds(at, 128)]


def attend_kernel(step, place, q_ref, kv_ref, out_ref, best, acc, held, peak, todo):
    half, y, z = place[0], place[1], place[2]
    own_row = 4 * half + y
    kv_rows = (own_row, 7 - own_row)
    back = lax.rem(y - step + 4, 4)
    q_rows = (4 * half + back, 4 * (1 - half) + back)

    def keys_of(tile):
        _, row, pair = tile
        at = 4 * row + 2 * pair
        return jnp.concatenate([kv_ref[at + part, :BLOCK] for part in range(2)], axis=0)

    def values_of(tile):
        _, row, pair = tile
        at = 4 * row + 2 * pair
        flipped = [
            kv_ref[at + part, BLOCK + piece * 128 : BLOCK + (piece + 1) * 128]
            for part in range(2)
            for piece in range(4)
        ]
        ones = jnp.ones((EXT - HEAD_DIM, 2 * BLOCK), jnp.bfloat16)
        return jnp.concatenate([jnp.concatenate(flipped, axis=1), ones], axis=0)

    def score(tile, keys, strip, mask=None):
        part = lax.dot_general(
            keys,
            q_ref[tile[0], strip * STRIP : (strip + 1) * STRIP],
            CONTRACT_LAST,
            preferred_element_type=jnp.float32,
        )
        if mask is not None:
            part = mask(part, strip)
        held[strip] = part
        peak[strip] = jnp.max(part, axis=0, keepdims=True)

    def update(tile, values, strip):
        slot = tile[0]
        old = best[slot, strip]
        new = jnp.maximum(old, peak[strip])
        weights = jnp.exp2(held[strip] * SCALE - new * SCALE)
        rescale = jnp.exp2((old - new) * SCALE)
        best[slot, strip] = new
        acc[slot, strip] = acc[slot, strip] * rescale + jnp.dot(
            values, weights.astype(jnp.bfloat16), preferred_element_type=jnp.float32
        )

    best[...] = jnp.full_like(best, LOWEST)
    acc[...] = jnp.zeros_like(acc)
    todo[0] = 0
    for slot in range(2):
        for row in range(2):

            @pl.when(kv_rows[row] < q_rows[slot])
            def _():
                count = todo[0]
                todo[1 + count] = 2 * slot + row
                todo[0] = count + 1

    def tile_at(at):
        entry = todo[1 + at // 2]
        return entry // 2, entry % 2, at % 2

    count = 2 * todo[0]

    @pl.when(count > 0)
    def _():
        start = tile_at(0)
        keys = keys_of(start)
        for strip in range(STRIPS):
            score(start, keys, strip)

        def step_on(at):
            now, later = tile_at(at), tile_at(at + 1)
            values, keys = values_of(now), keys_of(later)
            for strip in range(STRIPS):
                update(now, values, strip)
                score(later, keys, strip)

        def one(at, _):
            step_on(2 * at)
            step_on(2 * at + 1)
            return 0

        lax.fori_loop(0, todo[0] - 1, one, 0)
        step_on(count - 2)
        last = tile_at(count - 1)
        values = values_of(last)
        for strip in range(STRIPS):
            update(last, values, strip)

    def on_the_diagonal(slot, row):
        def causal(part, strip):
            key_at = lax.broadcasted_iota(jnp.int32, (BLOCK, STRIP), 0)
            token = lax.broadcasted_iota(jnp.int32, (BLOCK, STRIP), 1) + strip * STRIP % BLOCK
            near = jnp.where(key_at <= token, part[:BLOCK], LOWEST)
            return jnp.concatenate([near, jnp.where(z >= 1, part[BLOCK:], LOWEST)], axis=0)

        def far(part, strip):
            return jnp.concatenate(
                [jnp.where(z >= 3, part[:BLOCK], LOWEST), part[BLOCK:]], axis=0
            )

        def alone(pair, mask):
            tile = (slot, row, pair)
            keys, values = keys_of(tile), values_of(tile)
            for strip in range(STRIPS):
                score(tile, keys, strip, mask)
            for strip in range(STRIPS):
                update(tile, values, strip)

        alone(0, causal)
        pl.when(z >= 2)(lambda: alone(1, far))

    if step == 0:
        on_the_diagonal(0, 0)
    if step % 2 == 1:
        pl.when(kv_rows[1] == q_rows[1])(lambda: on_the_diagonal(1, 1))

    index = lax.broadcasted_iota(jnp.int32, (EXT - HEAD_DIM, STRIP), 0)
    for slot in range(2):
        for strip in range(STRIPS):
            at = slice(strip * STRIP, (strip + 1) * STRIP)
            total = acc[slot, strip, HEAD_DIM : HEAD_DIM + 1]
            empty = total == 0.0
            inverse = 1.0 / jnp.where(empty, 1.0, total)
            out_ref[slot, :HEAD_DIM, at] = (acc[slot, strip, :HEAD_DIM] * inverse).astype(
                jnp.bfloat16
            )
            level = best[slot, strip] * SCALE + jnp.log2(jnp.where(empty, 1.0, total))
            high = level.astype(jnp.bfloat16).astype(jnp.float32)
            middle = (level - high).astype(jnp.bfloat16).astype(jnp.float32)
            low = level - high - middle
            rows = jnp.where(index == 0, high, jnp.where(index == 1, middle, low))
            out_ref[slot, HEAD_DIM:, at] = rows.astype(jnp.bfloat16)


def attend(step, place, queries, blocks):
    return pl.pallas_call(
        functools.partial(attend_kernel, step),
        out_shape=jax.ShapeDtypeStruct((2, EXT, ROWS), jnp.bfloat16),
        in_specs=[smem()] + vmem(2),
        out_specs=vmem(1)[0],
        scratch_shapes=[
            pltpu.VMEM((2, STRIPS, 1, STRIP), jnp.float32),
            pltpu.VMEM((2, STRIPS, EXT, STRIP), jnp.float32),
            pltpu.VMEM((STRIPS, 2 * BLOCK, STRIP), jnp.float32),
            pltpu.VMEM((STRIPS, 1, STRIP), jnp.float32),
            pltpu.SMEM((8,), jnp.int32),
        ],
        compiler_params=PARAMS,
        name=f"attend{step}",
    )(place, queries, blocks)


def merge_kernel(place, *refs):
    parts, out_ref = refs[:4], refs[4]
    half = place[0]
    for slot in range(2):
        levels = []
        for part in parts:
            tail = part[slot, HEAD_DIM:].astype(jnp.float32)
            levels.append(tail[0:1] + tail[1:2] + tail[2:3])
        top = jnp.maximum(jnp.maximum(levels[0], levels[1]), jnp.maximum(levels[2], levels[3]))
        shares = [jnp.exp2(level - top) for level in levels]
        inverse = 1.0 / (shares[0] + shares[1] + shares[2] + shares[3])
        mixed = sum(
            part[slot, :HEAD_DIM].astype(jnp.float32) * (share * inverse)
            for part, share in zip(parts, shares)
        )
        row_half = half if slot == 0 else 1 - half
        for sub in range(2):
            for piece in range(4):
                at = sub * BLOCK + piece * 128
                out_ref[piece, row_half, :, sub * 128 : (sub + 1) * 128] = (
                    mixed[:, at : at + 128].T.astype(jnp.bfloat16)
                )


def pinned(value):
    return pltpu.with_memory_space_constraint(value, pltpu.HBM)


def ring(value, axis, steps):
    size = lax.axis_size(axis)
    return lax.ppermute(value, axis, [(at, (at + steps) % size) for at in range(size)])


def routed(value, target):
    pairs = []
    for half in range(2):
        for y in range(4):
            to_half, to_y = target(half, y)
            pairs.append((4 * half + y, 4 * to_half + to_y))
    return lax.ppermute(value, ("xl", "y"), pairs)


def on_device(query_rows, key_rows, value_rows):
    half, y, z = lax.axis_index("xl"), lax.axis_index("y"), lax.axis_index("z")
    place = jnp.stack([half, y, z]).astype(jnp.int32)
    message = jax.ShapeDtypeStruct((ROWS, 128), jnp.bfloat16)
    kv_other, q_other, kv_own, q_own = pl.pallas_call(
        pack_kernel,
        out_shape=(message,) * 4,
        in_specs=[smem()] + [pl.BlockSpec(memory_space=pltpu.HBM)] * 3,
        out_specs=tuple(vmem(4)),
        scratch_shapes=[
            pltpu.VMEM((BLOCK, 512), jnp.bfloat16),
            pltpu.VMEM((BLOCK, 256), jnp.bfloat16),
            pltpu.VMEM((BLOCK, 256), jnp.bfloat16),
            pltpu.SemaphoreType.DMA((3,)),
        ],
        compiler_params=PARAMS,
        name="pack",
    )(place, pinned(query_rows), pinned(key_rows), pinned(value_rows))
    kv_mirror = routed(kv_other, lambda h, r: (1 - h, 3 - r))
    q_swap = ring(q_other, "xl", 1)
    q_early = ring(q_own, "y", 3)
    q_swap, q_early = lax.optimization_barrier((q_swap, q_early))
    kv_pair = jnp.stack([kv_own, kv_mirror])
    pairs = {0: kv_pair}
    pairs |= {k: ring(kv_pair, "z", k) for k in (2, 3, 1)}
    blocks = jnp.concatenate(
        [pairs[k][row : row + 1] for row in range(2) for k in (0, 1, 3, 2)], axis=0
    )
    q_pair = jnp.stack([q_own, q_swap])
    queries = {0: q_pair}
    queries[1] = ring(q_pair, "y", 1)
    queries[3] = jnp.stack([q_early, ring(q_swap, "y", 3)])
    queries[2] = ring(q_pair, "y", 2)
    parts = [ring(attend(k, place, queries[k], blocks), "y", 4 - k) for k in (1, 3, 2)]
    parts.append(attend(0, place, queries[0], blocks))
    merged = pl.pallas_call(
        merge_kernel,
        out_shape=jax.ShapeDtypeStruct((4, 2, 128, 256), jnp.bfloat16),
        in_specs=[smem()] + vmem(4),
        out_specs=vmem(1)[0],
        compiler_params=PARAMS,
        name="merge",
    )(place, *parts)
    merged = merged.reshape(8, 128, 256)
    spread = lax.all_to_all(merged, ("xh", "core", "xl"), split_axis=0, concat_axis=0, tiled=True)
    return spread.transpose(1, 0, 2).reshape(128, 2048)


def solution(mesh):
    fine = Mesh(mesh.devices.reshape(2, 4, 4, 2, 2), ("xl", "y", "z", "xh", "core"))
    tokens, heads = ("xl", "y", "z"), ("xh", "core")
    return jax.shard_map(
        on_device,
        mesh=fine,
        in_specs=(P(tokens, heads),) * 3,
        out_specs=P(tokens + heads, None),
        check_vma=False,
    )
```

```python
import functools

import jax
import jax.numpy as jnp
from jax import lax
from jax.experimental import pallas as pl
from jax.experimental.pallas import tpu as pltpu
from jax.sharding import Mesh, PartitionSpec as P

HEAD_DIM = 128
SCALAR = 168
SCALE = SCALAR ** (-0.5) * 1.4426950408889634
LOWEST = -1e30
BLOCK = 512
ROWS = 2 * BLOCK
EXT = HEAD_DIM + 16
STRIP = 256
STRIPS = ROWS // STRIP

CONTRACT_LAST = (((1,), (1,)), ((), ()))
PARAMS = pltpu.CompilerParams(vmem_limit_bytes=30 * 2**20)


def vmem(count):
    return [pl.BlockSpec(memory_space=pltpu.VMEM)] * count


def smem():
    return pl.BlockSpec(memory_space=pltpu.SMEM)


def pack_kernel(
    place, query_in, key_in, value_in, kv_other, q_other, kv_own, q_own, query_ref, key_ref, value_ref, done
):
    half = place[0]
    copies = [
        pltpu.make_async_copy(key_in, key_ref, done.at[0]),
        pltpu.make_async_copy(value_in, value_ref, done.at[1]),
        pltpu.make_async_copy(query_in, query_ref, done.at[2]),
    ]
    for copy in copies:
        copy.start()
    copies[0].wait()
    for head, kv_out in ((1 - half, kv_other), (half, kv_own)):
        at = pl.multiple_of(head * 128, 128)
        kv_out[:BLOCK] = key_ref[:, pl.ds(at, 128)]
    copies[1].wait()
    for head, kv_out in ((1 - half, kv_other), (half, kv_own)):
        at = pl.multiple_of(head * 128, 128)
        for part in range(4):
            rows = value_ref[part * 128 : (part + 1) * 128, pl.ds(at, 128)]
            kv_out[BLOCK + part * 128 : BLOCK + (part + 1) * 128] = (
                rows.astype(jnp.float32).T.astype(jnp.bfloat16)
            )
    copies[2].wait()
    for head, q_out in ((1 - half, q_other), (half, q_own)):
        for part in range(2):
            at = pl.multiple_of(head * 256 + part * 128, 128)
            q_out[part * BLOCK : (part + 1) * BLOCK] = query_ref[:, pl.ds(at, 128)]


def attend_kernel(step, place, q_ref, kv_ref, out_ref, best, acc, held, peak, todo):
    half, y, z = place[0], place[1], place[2]
    own_row = 4 * half + y
    kv_rows = (own_row, 7 - own_row)
    back = lax.rem(y - step + 4, 4)
    q_rows = (4 * half + back, 4 * (1 - half) + back)

    def keys_of(tile):
        _, row, pair = tile
        at = 4 * row + 2 * pair
        return jnp.concatenate([kv_ref[at + part, :BLOCK] for part in range(2)], axis=0)

    def values_of(tile):
        _, row, pair = tile
        at = 4 * row + 2 * pair
        flipped = [
            kv_ref[at + part, BLOCK + piece * 128 : BLOCK + (piece + 1) * 128]
            for part in range(2)
            for piece in range(4)
        ]
        ones = jnp.ones((EXT - HEAD_DIM, 2 * BLOCK), jnp.bfloat16)
        return jnp.concatenate([jnp.concatenate(flipped, axis=1), ones], axis=0)

    def score(tile, keys, strip, mask=None):
        part = lax.dot_general(
            keys,
            q_ref[tile[0], strip * STRIP : (strip + 1) * STRIP],
            CONTRACT_LAST,
            preferred_element_type=jnp.float32,
        )
        if mask is not None:
            part = mask(part, strip)
        held[strip] = part
        peak[strip] = jnp.max(part, axis=0, keepdims=True)

    def update(tile, values, strip):
        slot = tile[0]
        old = best[slot, strip]
        new = jnp.maximum(old, peak[strip])
        weights = jnp.exp2(held[strip] * SCALE - new * SCALE)
        rescale = jnp.exp2((old - new) * SCALE)
        best[slot, strip] = new
        acc[slot, strip] = acc[slot, strip] * rescale + jnp.dot(
            values, weights.astype(jnp.bfloat16), preferred_element_type=jnp.float32
        )

    best[...] = jnp.full_like(best, LOWEST)
    acc[...] = jnp.zeros_like(acc)
    todo[0] = 0
    for slot in range(2):
        for row in range(2):

            @pl.when(kv_rows[row] < q_rows[slot])
            def _():
                count = todo[0]
                todo[1 + count] = 2 * slot + row
                todo[0] = count + 1

    def tile_at(at):
        entry = todo[1 + at // 2]
        return entry // 2, entry % 2, at % 2

    count = 2 * todo[0]

    @pl.when(count > 0)
    def _():
        start = tile_at(0)
        keys = keys_of(start)
        for strip in range(STRIPS):
            score(start, keys, strip)

        def step_on(at):
            now, later = tile_at(at), tile_at(at + 1)
            values, keys = values_of(now), keys_of(later)
            for strip in range(STRIPS):
                update(now, values, strip)
                score(later, keys, strip)

        def one(at, _):
            step_on(2 * at)
            step_on(2 * at + 1)
            return 0

        lax.fori_loop(0, todo[0] - 1, one, 0)
        step_on(count - 2)
        last = tile_at(count - 1)
        values = values_of(last)
        for strip in range(STRIPS):
            update(last, values, strip)

    def on_the_diagonal(slot, row):
        def causal(part, strip):
            key_at = lax.broadcasted_iota(jnp.int32, (BLOCK, STRIP), 0)
            token = lax.broadcasted_iota(jnp.int32, (BLOCK, STRIP), 1) + strip * STRIP % BLOCK
            near = jnp.where(key_at <= token, part[:BLOCK], LOWEST)
            return jnp.concatenate([near, jnp.where(z >= 1, part[BLOCK:], LOWEST)], axis=0)

        def far(part, strip):
            return jnp.concatenate(
                [jnp.where(z >= 3, part[:BLOCK], LOWEST), part[BLOCK:]], axis=0
            )

        def alone(pair, mask):
            tile = (slot, row, pair)
            keys, values = keys_of(tile), values_of(tile)
            for strip in range(STRIPS):
                score(tile, keys, strip, mask)
            for strip in range(STRIPS):
                update(tile, values, strip)

        alone(0, causal)
        pl.when(z >= 2)(lambda: alone(1, far))

    if step == 0:
        on_the_diagonal(0, 0)
    if step % 2 == 1:
        pl.when(kv_rows[1] == q_rows[1])(lambda: on_the_diagonal(1, 1))

    index = lax.broadcasted_iota(jnp.int32, (EXT - HEAD_DIM, STRIP), 0)
    for slot in range(2):
        for strip in range(STRIPS):
            at = slice(strip * STRIP, (strip + 1) * STRIP)
            total = acc[slot, strip, HEAD_DIM : HEAD_DIM + 1]
            empty = total == 0.0
            inverse = 1.0 / jnp.where(empty, 1.0, total)
            out_ref[slot, :HEAD_DIM, at] = (acc[slot, strip, :HEAD_DIM] * inverse).astype(
                jnp.bfloat16
            )
            level = best[slot, strip] * SCALE + jnp.log2(jnp.where(empty, 1.0, total))
            high = level.astype(jnp.bfloat16).astype(jnp.float32)
            middle = (level - high).astype(jnp.bfloat16).astype(jnp.float32)
            low = level - high - middle
            rows = jnp.where(index == 0, high, jnp.where(index == 1, middle, low))
            out_ref[slot, HEAD_DIM:, at] = rows.astype(jnp.bfloat16)


def attend(step, place, queries, blocks):
    return pl.pallas_call(
        functools.partial(attend_kernel, step),
        out_shape=jax.ShapeDtypeStruct((2, EXT, ROWS), jnp.bfloat16),
        in_specs=[smem()] + vmem(2),
        out_specs=vmem(1)[0],
        scratch_shapes=[
            pltpu.VMEM((2, STRIPS, 1, STRIP), jnp.float32),
            pltpu.VMEM((2, STRIPS, EXT, STRIP), jnp.float32),
            pltpu.VMEM((STRIPS, 2 * BLOCK, STRIP), jnp.float32),
            pltpu.VMEM((STRIPS, 1, STRIP), jnp.float32),
            pltpu.SMEM((8,), jnp.int32),
        ],
        compiler_params=PARAMS,
        name=f"attend{step}",
    )(place, queries, blocks)


def merge_kernel(place, *refs):
    parts, out_ref = refs[:4], refs[4]
    half = place[0]
    for slot in range(2):
        levels = []
        for part in parts:
            tail = part[slot, HEAD_DIM:].astype(jnp.float32)
            levels.append(tail[0:1] + tail[1:2] + tail[2:3])
        top = jnp.maximum(jnp.maximum(levels[0], levels[1]), jnp.maximum(levels[2], levels[3]))
        shares = [jnp.exp2(level - top) for level in levels]
        inverse = 1.0 / (shares[0] + shares[1] + shares[2] + shares[3])
        mixed = sum(
            part[slot, :HEAD_DIM].astype(jnp.float32) * (share * inverse)
            for part, share in zip(parts, shares)
        )
        row_half = half if slot == 0 else 1 - half
        for sub in range(2):
            for piece in range(4):
                at = sub * BLOCK + piece * 128
                out_ref[piece, row_half, :, sub * 128 : (sub + 1) * 128] = (
                    mixed[:, at : at + 128].T.astype(jnp.bfloat16)
                )


def pinned(value):
    return pltpu.with_memory_space_constraint(value, pltpu.HBM)


def ring(value, axis, steps):
    size = lax.axis_size(axis)
    return lax.ppermute(value, axis, [(at, (at + steps) % size) for at in range(size)])


def routed(value, target):
    pairs = []
    for half in range(2):
        for y in range(4):
            to_half, to_y = target(half, y)
            pairs.append((4 * half + y, 4 * to_half + to_y))
    return lax.ppermute(value, ("xl", "y"), pairs)


def on_device(query_rows, key_rows, value_rows):
    half, y, z = lax.axis_index("xl"), lax.axis_index("y"), lax.axis_index("z")
    place = jnp.stack([half, y, z]).astype(jnp.int32)
    message = jax.ShapeDtypeStruct((ROWS, 128), jnp.bfloat16)
    kv_other, q_other, kv_own, q_own = pl.pallas_call(
        pack_kernel,
        out_shape=(message,) * 4,
        in_specs=[smem()] + [pl.BlockSpec(memory_space=pltpu.HBM)] * 3,
        out_specs=tuple(vmem(4)),
        scratch_shapes=[
            pltpu.VMEM((BLOCK, 512), jnp.bfloat16),
            pltpu.VMEM((BLOCK, 256), jnp.bfloat16),
            pltpu.VMEM((BLOCK, 256), jnp.bfloat16),
            pltpu.SemaphoreType.DMA((3,)),
        ],
        compiler_params=PARAMS,
        name="pack",
    )(place, pinned(query_rows), pinned(key_rows), pinned(value_rows))
    kv_mirror = routed(kv_other, lambda h, r: (1 - h, 3 - r))
    q_swap = ring(q_other, "xl", 1)
    q_early = ring(q_own, "y", 1)
    q_swap, q_early = lax.optimization_barrier((q_swap, q_early))
    kv_pair = jnp.stack([kv_own, kv_mirror])
    pairs = {0: kv_pair}
    pairs |= {k: ring(kv_pair, "z", k) for k in (2, 3, 1)}
    blocks = jnp.concatenate(
        [pairs[k][row : row + 1] for row in range(2) for k in (0, 1, 3, 2)], axis=0
    )
    q_pair = jnp.stack([q_own, q_swap])
    queries = {0: q_pair}
    queries[3] = ring(q_pair, "y", 3)
    queries[1] = jnp.stack([q_early, ring(q_swap, "y", 1)])
    queries[2] = ring(q_pair, "y", 2)
    parts = [ring(attend(k, place, queries[k], blocks), "y", 4 - k) for k in (3, 1, 2)]
    parts.append(attend(0, place, queries[0], blocks))
    merged = pl.pallas_call(
        merge_kernel,
        out_shape=jax.ShapeDtypeStruct((4, 2, 128, 256), jnp.bfloat16),
        in_specs=[smem()] + vmem(4),
        out_specs=vmem(1)[0],
        compiler_params=PARAMS,
        name="merge",
    )(place, *parts)
    merged = merged.reshape(8, 128, 256)
    spread = lax.all_to_all(merged, ("xh", "core", "xl"), split_axis=0, concat_axis=0, tiled=True)
    return spread.transpose(1, 0, 2).reshape(128, 2048)


def solution(mesh):
    fine = Mesh(mesh.devices.reshape(2, 4, 4, 2, 2), ("xl", "y", "z", "xh", "core"))
    tokens, heads = ("xl", "y", "z"), ("xh", "core")
    return jax.shard_map(
        on_device,
        mesh=fine,
        in_specs=(P(tokens, heads),) * 3,
        out_specs=P(tokens + heads, None),
        check_vma=False,
    )
```

```python
import functools

import jax
import jax.numpy as jnp
from jax import lax
from jax.experimental import pallas as pl
from jax.experimental.pallas import tpu as pltpu
from jax.sharding import Mesh, PartitionSpec as P

HEAD_DIM = 128
SCALAR = 168
SCALE = SCALAR ** (-0.5) * 1.4426950408889634
LOWEST = -1e30
BLOCK = 512
ROWS = 2 * BLOCK
EXT = HEAD_DIM + 16
STRIP = 256
STRIPS = ROWS // STRIP

CONTRACT_LAST = (((1,), (1,)), ((), ()))
PARAMS = pltpu.CompilerParams(vmem_limit_bytes=30 * 2**20)


def vmem(count):
    return [pl.BlockSpec(memory_space=pltpu.VMEM)] * count


def smem():
    return pl.BlockSpec(memory_space=pltpu.SMEM)


def pack_kernel(
    place, query_in, key_in, value_in, kv_other, q_other, kv_own, q_own, query_ref, key_ref, value_ref, done
):
    half = place[0]
    copies = [
        pltpu.make_async_copy(key_in, key_ref, done.at[0]),
        pltpu.make_async_copy(value_in, value_ref, done.at[1]),
        pltpu.make_async_copy(query_in, query_ref, done.at[2]),
    ]
    for copy in copies:
        copy.start()
    copies[0].wait()
    for head, kv_out in ((1 - half, kv_other), (half, kv_own)):
        at = pl.multiple_of(head * 128, 128)
        kv_out[:BLOCK] = key_ref[:, pl.ds(at, 128)]
    copies[1].wait()
    for head, kv_out in ((1 - half, kv_other), (half, kv_own)):
        at = pl.multiple_of(head * 128, 128)
        for part in range(4):
            rows = value_ref[part * 128 : (part + 1) * 128, pl.ds(at, 128)]
            kv_out[BLOCK + part * 128 : BLOCK + (part + 1) * 128] = (
                rows.astype(jnp.float32).T.astype(jnp.bfloat16)
            )
    copies[2].wait()
    for head, q_out in ((1 - half, q_other), (half, q_own)):
        for part in range(2):
            at = pl.multiple_of(head * 256 + part * 128, 128)
            q_out[part * BLOCK : (part + 1) * BLOCK] = query_ref[:, pl.ds(at, 128)]


def attend_kernel(step, place, q_ref, kv_ref, out_ref, best, acc, held, peak, todo):
    half, y, z = place[0], place[1], place[2]
    own_row = 4 * half + y
    kv_rows = (own_row, 7 - own_row)
    back = lax.rem(y - step + 4, 4)
    q_rows = (4 * half + back, 4 * (1 - half) + back)

    def keys_of(tile):
        _, row, pair = tile
        at = 4 * row + 2 * pair
        return jnp.concatenate([kv_ref[at + part, :BLOCK] for part in range(2)], axis=0)

    def values_of(tile):
        _, row, pair = tile
        at = 4 * row + 2 * pair
        flipped = [
            kv_ref[at + part, BLOCK + piece * 128 : BLOCK + (piece + 1) * 128]
            for part in range(2)
            for piece in range(4)
        ]
        ones = jnp.ones((EXT - HEAD_DIM, 2 * BLOCK), jnp.bfloat16)
        return jnp.concatenate([jnp.concatenate(flipped, axis=1), ones], axis=0)

    def score(tile, keys, strip, mask=None):
        part = lax.dot_general(
            keys,
            q_ref[tile[0], strip * STRIP : (strip + 1) * STRIP],
            CONTRACT_LAST,
            preferred_element_type=jnp.float32,
        )
        if mask is not None:
            part = mask(part, strip)
        held[strip] = part
        peak[strip] = jnp.max(part, axis=0, keepdims=True)

    def update(tile, values, strip):
        slot = tile[0]
        old = best[slot, strip]
        new = jnp.maximum(old, peak[strip])
        weights = jnp.exp2(held[strip] * SCALE - new * SCALE)
        rescale = jnp.exp2((old - new) * SCALE)
        best[slot, strip] = new
        acc[slot, strip] = acc[slot, strip] * rescale + jnp.dot(
            values, weights.astype(jnp.bfloat16), preferred_element_type=jnp.float32
        )

    best[...] = jnp.full_like(best, LOWEST)
    acc[...] = jnp.zeros_like(acc)
    todo[0] = 0
    for slot in range(2):
        for row in range(2):

            @pl.when(kv_rows[row] < q_rows[slot])
            def _():
                count = todo[0]
                todo[1 + count] = 2 * slot + row
                todo[0] = count + 1

    def tile_at(at):
        entry = todo[1 + at // 2]
        return entry // 2, entry % 2, at % 2

    count = 2 * todo[0]

    @pl.when(count > 0)
    def _():
        start = tile_at(0)
        keys = keys_of(start)
        for strip in range(STRIPS):
            score(start, keys, strip)

        def step_on(at):
            now, later = tile_at(at), tile_at(at + 1)
            values, keys = values_of(now), keys_of(later)
            for strip in range(STRIPS):
                update(now, values, strip)
                score(later, keys, strip)

        def one(at, _):
            step_on(2 * at)
            step_on(2 * at + 1)
            return 0

        lax.fori_loop(0, todo[0] - 1, one, 0)
        step_on(count - 2)
        last = tile_at(count - 1)
        values = values_of(last)
        for strip in range(STRIPS):
            update(last, values, strip)

    def on_the_diagonal(slot, row):
        def causal(part, strip):
            key_at = lax.broadcasted_iota(jnp.int32, (BLOCK, STRIP), 0)
            token = lax.broadcasted_iota(jnp.int32, (BLOCK, STRIP), 1) + strip * STRIP % BLOCK
            near = jnp.where(key_at <= token, part[:BLOCK], LOWEST)
            return jnp.concatenate([near, jnp.where(z >= 1, part[BLOCK:], LOWEST)], axis=0)

        def far(part, strip):
            return jnp.concatenate(
                [jnp.where(z >= 3, part[:BLOCK], LOWEST), part[BLOCK:]], axis=0
            )

        near_tile, far_tile = (slot, row, 0), (slot, row, 1)
        keys = keys_of(near_tile)
        for strip in range(STRIPS):
            score(near_tile, keys, strip, causal)

        @pl.when(z >= 2)
        def _():
            values, keys = values_of(near_tile), keys_of(far_tile)
            for strip in range(STRIPS):
                update(near_tile, values, strip)
                score(far_tile, keys, strip, far)
            values = values_of(far_tile)
            for strip in range(STRIPS):
                update(far_tile, values, strip)

        @pl.when(z < 2)
        def _():
            values = values_of(near_tile)
            for strip in range(STRIPS):
                update(near_tile, values, strip)

    if step == 0:
        on_the_diagonal(0, 0)
    if step % 2 == 1:
        pl.when(kv_rows[1] == q_rows[1])(lambda: on_the_diagonal(1, 1))

    index = lax.broadcasted_iota(jnp.int32, (EXT - HEAD_DIM, STRIP), 0)
    for slot in range(2):
        for strip in range(STRIPS):
            at = slice(strip * STRIP, (strip + 1) * STRIP)
            total = acc[slot, strip, HEAD_DIM : HEAD_DIM + 1]
            empty = total == 0.0
            inverse = 1.0 / jnp.where(empty, 1.0, total)
            out_ref[slot, :HEAD_DIM, at] = (acc[slot, strip, :HEAD_DIM] * inverse).astype(
                jnp.bfloat16
            )
            level = best[slot, strip] * SCALE + jnp.log2(jnp.where(empty, 1.0, total))
            high = level.astype(jnp.bfloat16).astype(jnp.float32)
            middle = (level - high).astype(jnp.bfloat16).astype(jnp.float32)
            low = level - high - middle
            rows = jnp.where(index == 0, high, jnp.where(index == 1, middle, low))
            out_ref[slot, HEAD_DIM:, at] = rows.astype(jnp.bfloat16)


def attend(step, place, queries, blocks):
    return pl.pallas_call(
        functools.partial(attend_kernel, step),
        out_shape=jax.ShapeDtypeStruct((2, EXT, ROWS), jnp.bfloat16),
        in_specs=[smem()] + vmem(2),
        out_specs=vmem(1)[0],
        scratch_shapes=[
            pltpu.VMEM((2, STRIPS, 1, STRIP), jnp.float32),
            pltpu.VMEM((2, STRIPS, EXT, STRIP), jnp.float32),
            pltpu.VMEM((STRIPS, 2 * BLOCK, STRIP), jnp.float32),
            pltpu.VMEM((STRIPS, 1, STRIP), jnp.float32),
            pltpu.SMEM((8,), jnp.int32),
        ],
        compiler_params=PARAMS,
        name=f"attend{step}",
    )(place, queries, blocks)


def merge_kernel(place, *refs):
    parts, out_ref = refs[:4], refs[4]
    half = place[0]
    for slot in range(2):
        levels = []
        for part in parts:
            tail = part[slot, HEAD_DIM:].astype(jnp.float32)
            levels.append(tail[0:1] + tail[1:2] + tail[2:3])
        top = jnp.maximum(jnp.maximum(levels[0], levels[1]), jnp.maximum(levels[2], levels[3]))
        shares = [jnp.exp2(level - top) for level in levels]
        inverse = 1.0 / (shares[0] + shares[1] + shares[2] + shares[3])
        mixed = sum(
            part[slot, :HEAD_DIM].astype(jnp.float32) * (share * inverse)
            for part, share in zip(parts, shares)
        )
        row_half = half if slot == 0 else 1 - half
        for sub in range(2):
            for piece in range(4):
                at = sub * BLOCK + piece * 128
                out_ref[piece, row_half, :, sub * 128 : (sub + 1) * 128] = (
                    mixed[:, at : at + 128].T.astype(jnp.bfloat16)
                )


def pinned(value):
    return pltpu.with_memory_space_constraint(value, pltpu.HBM)


def ring(value, axis, steps):
    size = lax.axis_size(axis)
    return lax.ppermute(value, axis, [(at, (at + steps) % size) for at in range(size)])


def routed(value, target):
    pairs = []
    for half in range(2):
        for y in range(4):
            to_half, to_y = target(half, y)
            pairs.append((4 * half + y, 4 * to_half + to_y))
    return lax.ppermute(value, ("xl", "y"), pairs)


def on_device(query_rows, key_rows, value_rows):
    half, y, z = lax.axis_index("xl"), lax.axis_index("y"), lax.axis_index("z")
    place = jnp.stack([half, y, z]).astype(jnp.int32)
    message = jax.ShapeDtypeStruct((ROWS, 128), jnp.bfloat16)
    kv_other, q_other, kv_own, q_own = pl.pallas_call(
        pack_kernel,
        out_shape=(message,) * 4,
        in_specs=[smem()] + [pl.BlockSpec(memory_space=pltpu.HBM)] * 3,
        out_specs=tuple(vmem(4)),
        scratch_shapes=[
            pltpu.VMEM((BLOCK, 512), jnp.bfloat16),
            pltpu.VMEM((BLOCK, 256), jnp.bfloat16),
            pltpu.VMEM((BLOCK, 256), jnp.bfloat16),
            pltpu.SemaphoreType.DMA((3,)),
        ],
        compiler_params=PARAMS,
        name="pack",
    )(place, pinned(query_rows), pinned(key_rows), pinned(value_rows))
    kv_mirror = routed(kv_other, lambda h, r: (1 - h, 3 - r))
    q_swap = ring(q_other, "xl", 1)
    q_early = ring(q_own, "y", 1)
    q_swap, q_early = lax.optimization_barrier((q_swap, q_early))
    kv_pair = jnp.stack([kv_own, kv_mirror])
    pairs = {0: kv_pair}
    pairs |= {k: ring(kv_pair, "z", k) for k in (2, 3, 1)}
    blocks = jnp.concatenate(
        [pairs[k][row : row + 1] for row in range(2) for k in (0, 1, 3, 2)], axis=0
    )
    q_pair = jnp.stack([q_own, q_swap])
    queries = {0: q_pair}
    queries[3] = ring(q_pair, "y", 3)
    queries[1] = jnp.stack([q_early, ring(q_swap, "y", 1)])
    queries[2] = ring(q_pair, "y", 2)
    parts = [ring(attend(k, place, queries[k], blocks), "y", 4 - k) for k in (3, 1, 2)]
    parts.append(attend(0, place, queries[0], blocks))
    merged = pl.pallas_call(
        merge_kernel,
        out_shape=jax.ShapeDtypeStruct((4, 2, 128, 256), jnp.bfloat16),
        in_specs=[smem()] + vmem(4),
        out_specs=vmem(1)[0],
        compiler_params=PARAMS,
        name="merge",
    )(place, *parts)
    merged = merged.reshape(8, 128, 256)
    spread = lax.all_to_all(merged, ("xh", "core", "xl"), split_axis=0, concat_axis=0, tiled=True)
    return spread.transpose(1, 0, 2).reshape(128, 2048)


def solution(mesh):
    fine = Mesh(mesh.devices.reshape(2, 4, 4, 2, 2), ("xl", "y", "z", "xh", "core"))
    tokens, heads = ("xl", "y", "z"), ("xh", "core")
    return jax.shard_map(
        on_device,
        mesh=fine,
        in_specs=(P(tokens, heads),) * 3,
        out_specs=P(tokens + heads, None),
        check_vma=False,
    )
```

```python
import functools

import jax
import jax.numpy as jnp
from jax import lax
from jax.experimental import pallas as pl
from jax.experimental.pallas import tpu as pltpu
from jax.sharding import Mesh, PartitionSpec as P

HEAD_DIM = 128
SCALAR = 168
SCALE = SCALAR ** (-0.5) * 1.4426950408889634
LOWEST = -1e30
BLOCK = 512
ROWS = 2 * BLOCK
EXT = HEAD_DIM + 16
STRIP = 256
STRIPS = ROWS // STRIP

CONTRACT_LAST = (((1,), (1,)), ((), ()))
PARAMS = pltpu.CompilerParams(vmem_limit_bytes=30 * 2**20)


def vmem(count):
    return [pl.BlockSpec(memory_space=pltpu.VMEM)] * count


def smem():
    return pl.BlockSpec(memory_space=pltpu.SMEM)


def pack_kernel(
    place, query_in, key_in, value_in, kv_other, q_other, kv_own, q_own, query_ref, key_ref, value_ref, done
):
    half = place[0]
    copies = [
        pltpu.make_async_copy(key_in, key_ref, done.at[0]),
        pltpu.make_async_copy(value_in, value_ref, done.at[1]),
        pltpu.make_async_copy(query_in, query_ref, done.at[2]),
    ]
    for copy in copies:
        copy.start()
    copies[0].wait()
    for head, kv_out in ((1 - half, kv_other), (half, kv_own)):
        at = pl.multiple_of(head * 128, 128)
        kv_out[:BLOCK] = key_ref[:, pl.ds(at, 128)]
    copies[1].wait()
    for head, kv_out in ((1 - half, kv_other), (half, kv_own)):
        at = pl.multiple_of(head * 128, 128)
        for part in range(4):
            rows = value_ref[part * 128 : (part + 1) * 128, pl.ds(at, 128)]
            kv_out[BLOCK + part * 128 : BLOCK + (part + 1) * 128] = (
                rows.astype(jnp.float32).T.astype(jnp.bfloat16)
            )
    copies[2].wait()
    for head, q_out in ((1 - half, q_other), (half, q_own)):
        for part in range(2):
            at = pl.multiple_of(head * 256 + part * 128, 128)
            q_out[part * BLOCK : (part + 1) * BLOCK] = query_ref[:, pl.ds(at, 128)]


def attend_kernel(step, place, q_ref, kv_ref, out_ref, best, acc, held, peak, todo):
    half, y, z = place[0], place[1], place[2]
    own_row = 4 * half + y
    kv_rows = (own_row, 7 - own_row)
    back = lax.rem(y - step + 4, 4)
    q_rows = (4 * half + back, 4 * (1 - half) + back)

    def keys_of(tile):
        _, row, pair = tile
        at = 4 * row + 2 * pair
        return jnp.concatenate([kv_ref[at + part, :BLOCK] for part in range(2)], axis=0)

    def values_of(tile):
        _, row, pair = tile
        at = 4 * row + 2 * pair
        flipped = [
            kv_ref[at + part, BLOCK + piece * 128 : BLOCK + (piece + 1) * 128]
            for part in range(2)
            for piece in range(4)
        ]
        ones = jnp.ones((EXT - HEAD_DIM, 2 * BLOCK), jnp.bfloat16)
        return jnp.concatenate([jnp.concatenate(flipped, axis=1), ones], axis=0)

    def score(tile, keys, strip, mask=None):
        part = lax.dot_general(
            keys,
            q_ref[tile[0], strip * STRIP : (strip + 1) * STRIP],
            CONTRACT_LAST,
            preferred_element_type=jnp.float32,
        )
        if mask is not None:
            part = mask(part, strip)
        held[strip] = part
        peak[strip] = jnp.max(part, axis=0, keepdims=True)

    def update(tile, values, strip):
        slot = tile[0]
        old = best[slot, strip]
        new = jnp.maximum(old, peak[strip])
        weights = jnp.exp2(held[strip] * SCALE - new * SCALE)
        rescale = jnp.exp2((old - new) * SCALE)
        best[slot, strip] = new
        acc[slot, strip] = acc[slot, strip] * rescale + jnp.dot(
            values, weights.astype(jnp.bfloat16), preferred_element_type=jnp.float32
        )

    best[...] = jnp.full_like(best, LOWEST)
    acc[...] = jnp.zeros_like(acc)
    todo[0] = 0
    for slot in range(2):
        for row in range(2):

            @pl.when(kv_rows[row] < q_rows[slot])
            def _():
                count = todo[0]
                todo[1 + count] = 2 * slot + row
                todo[0] = count + 1

    def tile_at(at):
        entry = todo[1 + at // 2]
        return entry // 2, entry % 2, at % 2

    count = 2 * todo[0]

    @pl.when(count > 0)
    def _():
        start = tile_at(0)
        keys = keys_of(start)
        for strip in range(STRIPS):
            score(start, keys, strip)

        def step_on(at):
            now, later = tile_at(at), tile_at(at + 1)
            values, keys = values_of(now), keys_of(later)
            for strip in range(STRIPS):
                update(now, values, strip)
                score(later, keys, strip)

        def one(at, _):
            step_on(2 * at)
            step_on(2 * at + 1)
            return 0

        lax.fori_loop(0, todo[0] - 1, one, 0)
        step_on(count - 2)
        last = tile_at(count - 1)
        values = values_of(last)
        for strip in range(STRIPS):
            update(last, values, strip)

    def on_the_diagonal(slot, row):
        def causal(part, strip):
            key_at = lax.broadcasted_iota(jnp.int32, (BLOCK, STRIP), 0)
            token = lax.broadcasted_iota(jnp.int32, (BLOCK, STRIP), 1) + strip * STRIP % BLOCK
            near = jnp.where(key_at <= token, part[:BLOCK], LOWEST)
            return jnp.concatenate([near, jnp.where(z >= 1, part[BLOCK:], LOWEST)], axis=0)

        def far(part, strip):
            return jnp.concatenate(
                [jnp.where(z >= 3, part[:BLOCK], LOWEST), part[BLOCK:]], axis=0
            )

        near_tile, far_tile = (slot, row, 0), (slot, row, 1)
        keys = keys_of(near_tile)
        for strip in range(STRIPS):
            score(near_tile, keys, strip, causal)

        @pl.when(z >= 2)
        def _():
            values, keys = values_of(near_tile), keys_of(far_tile)
            for strip in range(STRIPS):
                update(near_tile, values, strip)
                score(far_tile, keys, strip, far)
            values = values_of(far_tile)
            for strip in range(STRIPS):
                update(far_tile, values, strip)

        @pl.when(z < 2)
        def _():
            values = values_of(near_tile)
            for strip in range(STRIPS):
                update(near_tile, values, strip)

    if step == 0:
        on_the_diagonal(0, 0)
    if step % 2 == 1:
        pl.when(kv_rows[1] == q_rows[1])(lambda: on_the_diagonal(1, 1))

    index = lax.broadcasted_iota(jnp.int32, (EXT - HEAD_DIM, STRIP), 0)
    for strip in range(STRIPS):
        at = slice(strip * STRIP, (strip + 1) * STRIP)
        rows = jnp.zeros((EXT - HEAD_DIM, STRIP), jnp.float32)
        for slot in range(2):
            total = acc[slot, strip, HEAD_DIM : HEAD_DIM + 1]
            empty = total == 0.0
            inverse = 1.0 / jnp.where(empty, 1.0, total)
            out_ref[slot * HEAD_DIM : (slot + 1) * HEAD_DIM, at] = (
                acc[slot, strip, :HEAD_DIM] * inverse
            ).astype(jnp.bfloat16)
            level = best[slot, strip] * SCALE + jnp.log2(jnp.where(empty, 1.0, total))
            high = level.astype(jnp.bfloat16).astype(jnp.float32)
            middle = (level - high).astype(jnp.bfloat16).astype(jnp.float32)
            low = level - high - middle
            for place_at, value in enumerate((high, middle, low)):
                rows = jnp.where(index == 3 * slot + place_at, value, rows)
        out_ref[2 * HEAD_DIM :, at] = rows.astype(jnp.bfloat16)


def attend(step, place, queries, blocks):
    return pl.pallas_call(
        functools.partial(attend_kernel, step),
        out_shape=jax.ShapeDtypeStruct((HEAD_DIM + EXT, ROWS), jnp.bfloat16),
        in_specs=[smem()] + vmem(2),
        out_specs=vmem(1)[0],
        scratch_shapes=[
            pltpu.VMEM((2, STRIPS, 1, STRIP), jnp.float32),
            pltpu.VMEM((2, STRIPS, EXT, STRIP), jnp.float32),
            pltpu.VMEM((STRIPS, 2 * BLOCK, STRIP), jnp.float32),
            pltpu.VMEM((STRIPS, 1, STRIP), jnp.float32),
            pltpu.SMEM((8,), jnp.int32),
        ],
        compiler_params=PARAMS,
        name=f"attend{step}",
    )(place, queries, blocks)


def merge_kernel(place, *refs):
    parts, out_ref = refs[:4], refs[4]
    half = place[0]
    for slot in range(2):
        levels = []
        for part in parts:
            tail = part[2 * HEAD_DIM :].astype(jnp.float32)
            levels.append(sum(tail[3 * slot + at : 3 * slot + at + 1] for at in range(3)))
        top = jnp.maximum(jnp.maximum(levels[0], levels[1]), jnp.maximum(levels[2], levels[3]))
        shares = [jnp.exp2(level - top) for level in levels]
        inverse = 1.0 / (shares[0] + shares[1] + shares[2] + shares[3])
        mixed = sum(
            part[slot * HEAD_DIM : (slot + 1) * HEAD_DIM].astype(jnp.float32) * (share * inverse)
            for part, share in zip(parts, shares)
        )
        row_half = half if slot == 0 else 1 - half
        for sub in range(2):
            for piece in range(4):
                at = sub * BLOCK + piece * 128
                out_ref[piece, row_half, :, sub * 128 : (sub + 1) * 128] = (
                    mixed[:, at : at + 128].T.astype(jnp.bfloat16)
                )


def pinned(value):
    return pltpu.with_memory_space_constraint(value, pltpu.HBM)


def ring(value, axis, steps):
    size = lax.axis_size(axis)
    return lax.ppermute(value, axis, [(at, (at + steps) % size) for at in range(size)])


def routed(value, target):
    pairs = []
    for half in range(2):
        for y in range(4):
            to_half, to_y = target(half, y)
            pairs.append((4 * half + y, 4 * to_half + to_y))
    return lax.ppermute(value, ("xl", "y"), pairs)


def on_device(query_rows, key_rows, value_rows):
    half, y, z = lax.axis_index("xl"), lax.axis_index("y"), lax.axis_index("z")
    place = jnp.stack([half, y, z]).astype(jnp.int32)
    message = jax.ShapeDtypeStruct((ROWS, 128), jnp.bfloat16)
    kv_other, q_other, kv_own, q_own = pl.pallas_call(
        pack_kernel,
        out_shape=(message,) * 4,
        in_specs=[smem()] + [pl.BlockSpec(memory_space=pltpu.HBM)] * 3,
        out_specs=tuple(vmem(4)),
        scratch_shapes=[
            pltpu.VMEM((BLOCK, 512), jnp.bfloat16),
            pltpu.VMEM((BLOCK, 256), jnp.bfloat16),
            pltpu.VMEM((BLOCK, 256), jnp.bfloat16),
            pltpu.SemaphoreType.DMA((3,)),
        ],
        compiler_params=PARAMS,
        name="pack",
    )(place, pinned(query_rows), pinned(key_rows), pinned(value_rows))
    kv_mirror = routed(kv_other, lambda h, r: (1 - h, 3 - r))
    q_swap = ring(q_other, "xl", 1)
    q_early = ring(q_own, "y", 1)
    q_swap, q_early = lax.optimization_barrier((q_swap, q_early))
    kv_pair = jnp.stack([kv_own, kv_mirror])
    pairs = {0: kv_pair}
    pairs |= {k: ring(kv_pair, "z", k) for k in (2, 3, 1)}
    blocks = jnp.concatenate(
        [pairs[k][row : row + 1] for row in range(2) for k in (0, 1, 3, 2)], axis=0
    )
    q_pair = jnp.stack([q_own, q_swap])
    queries = {0: q_pair}
    queries[3] = ring(q_pair, "y", 3)
    queries[1] = jnp.stack([q_early, ring(q_swap, "y", 1)])
    queries[2] = ring(q_pair, "y", 2)
    parts = [ring(attend(k, place, queries[k], blocks), "y", 4 - k) for k in (3, 1, 2)]
    parts.append(attend(0, place, queries[0], blocks))
    merged = pl.pallas_call(
        merge_kernel,
        out_shape=jax.ShapeDtypeStruct((4, 2, 128, 256), jnp.bfloat16),
        in_specs=[smem()] + vmem(4),
        out_specs=vmem(1)[0],
        compiler_params=PARAMS,
        name="merge",
    )(place, *parts)
    merged = merged.reshape(8, 128, 256)
    spread = lax.all_to_all(merged, ("xh", "core", "xl"), split_axis=0, concat_axis=0, tiled=True)
    return spread.transpose(1, 0, 2).reshape(128, 2048)


def solution(mesh):
    fine = Mesh(mesh.devices.reshape(2, 4, 4, 2, 2), ("xl", "y", "z", "xh", "core"))
    tokens, heads = ("xl", "y", "z"), ("xh", "core")
    return jax.shard_map(
        on_device,
        mesh=fine,
        in_specs=(P(tokens, heads),) * 3,
        out_specs=P(tokens + heads, None),
        check_vma=False,
    )
```
